32 devices in a mesh: segment: 4 (over y, x), dom: 8 (over z, core).
Axes of the slice: x: 2, y: 2, z: 4, core: 2. Of those that a mesh axis runs over, the one named last changes fastest.
Arguments:
- states_in: bfloat16 [4, 4096, 512], P('segment', 'dom'), may hold values from -6 to 6
- states_mid: bfloat16 [4, 4096, 512], P('segment', 'dom'), may hold values from -6 to 6
- grad_out: bfloat16 [4, 4096, 512], P('segment', 'dom'), may hold values from -6 to 6
- w_in: bfloat16 [4, 2, 512, 512], P('segment'), may hold values from -0.25 to 0.25
- w_out: bfloat16 [4, 2, 512, 512], P('segment'), may hold values from -0.25 to 0.25
- tile_index: int32 [64, 2], P('dom'), may hold values from 0 to 3, as said below
- tile_values: bfloat16 [64, 128, 128], P('dom'), may hold values from -0.3125 to 0.3125
- tile_count: int32 [8], P('dom'), may hold values from 2 to 8, as said below
- coupling: bfloat16 [1536, 512], P('dom'), may hold values from -0.4375 to 0.4375
- bound_index: int32 [8, 3, 64], P('dom'), may hold values from 0 to 511
- bound_count: int32 [8, 3], P('dom'), may hold values from 1 to 64, as said below
Outputs:
- grad_prev: bfloat16 [4, 4096, 512], P('segment', 'dom')
The draws below stay inside these ranges and needn't reach their ends.
Inputs may be any that keep to these rules, and one draw needn't show every extreme that they name: `bound_count`: the value 64 is reached in every draw. Tile slots at or beyond tile_count are not used; 8 is reached by some partition in every draw. `tile_index`: within one partition no two tile slots have the same destination and source block.
All inputs are finite; a program needn't handle non-finite values.
Results may differ from the reference program's by a relative error of at most 0.008.
Values may be sent and summed in bfloat16 or wider, within the bound.
A program may use at most 64 MiB of HBM per device.

```python
import jax
import jax.numpy as jnp
from jax import lax

D = 512
BLOCK = 128
NODES_DEV = 512
TILES = 8
ROUNDS = 3
BOUND_ROWS = 64
LAYERS = 2
HALO = 192
PARTITIONS = 8
SECTIONS = 4
NODES = 4096


def draw_bound_count(key, part):
    key_a, key_b = jax.random.split(jax.random.fold_in(key, 4242))
    counts = jax.random.randint(key_a, (PARTITIONS, ROUNDS), 1, BOUND_ROWS + 1).astype(jnp.int32)
    where_full = jax.random.randint(key_b, (2,), 0, PARTITIONS * ROUNDS)
    flat = counts.reshape(PARTITIONS * ROUNDS).at[where_full].set(BOUND_ROWS)
    return flat.reshape(PARTITIONS, ROUNDS).astype(jnp.int32)


def draw_tile_count(key, part):
    key_a, key_b = jax.random.split(jax.random.fold_in(key, 99))
    counts = jax.random.randint(key_a, (PARTITIONS,), max(1, TILES // 4), TILES + 1).astype(jnp.int32)
    where_full = jax.random.randint(key_b, (), 0, PARTITIONS)
    return counts.at[where_full].set(TILES).astype(jnp.int32)


def draw_tile_index(key, part):
    blocks = NODES_DEV // BLOCK
    keys = jax.random.split(jax.random.fold_in(key, 777), PARTITIONS)

    def one_partition(sub):
        order = jax.random.permutation(sub, blocks * blocks)[:TILES].astype(jnp.int32)
        return jnp.stack([order // blocks, order % blocks], axis=1).astype(jnp.int32)
    pairs = jax.vmap(one_partition)(keys)
    return pairs.reshape(PARTITIONS * TILES, 2).astype(jnp.int32)


def with_ends(values, own_key, least, top_value):
    extent = values.shape
    spot = [jax.random.randint(jax.random.fold_in(own_key, axis), (), 0, extent[axis]) for axis in range(len(extent))]
    values = values.at[tuple(spot)].set(least)
    longest = extent.index(max(extent))
    spot[longest] = (spot[longest] + 1) % extent[longest]
    return values.at[tuple(spot)].set(top_value)


def level_of(key, extent, cuts, low, high):
    def one(dim, blocks):
        draws = jax.random.uniform(jax.random.fold_in(jax.random.fold_in(key, 6), dim), (blocks,), jnp.float32, low / len(cuts), high / len(cuts))
        return jnp.repeat(jnp.exp(draws), extent[dim] // blocks).reshape((-1,) + (1,) * (len(extent) - dim - 1))

    gain = one(*cuts[0])
    for cut in cuts[1:]:
        gain = gain * one(*cut)
    return gain


def bell_draw(rng, shape, spread, bound, shards=(), held_as=jnp.bfloat16):
    array = jax.random.normal(rng, shape, jnp.float32) * spread
    if len(shards) > 0:
        array = level_of(rng, shape, shards, -0.22, 0.18) * array
    return jnp.clip(array, min=-bound, max=bound).astype(held_as)


def setup_inputs(seed: int = 0) -> dict:
    seeds = jax.random.split(jax.random.key(seed), 12)
    states_in = bell_draw(seeds[0], (SECTIONS, NODES, D), 1.0, 6.0, ((0, 4), (1, 8)))
    states_mid = bell_draw(seeds[1], (SECTIONS, NODES, D), 1.0, 6.0, ((0, 4), (1, 8)))
    grad_out = bell_draw(seeds[2], (SECTIONS, NODES, D), 1.0, 6.0, ((0, 4), (1, 8)))
    w_in = bell_draw(seeds[3], (SECTIONS, LAYERS, D, D), D ** -0.5, 0.25, ((0, 4),))
    w_out = bell_draw(seeds[4], (SECTIONS, LAYERS, D, D), D ** -0.5, 0.25, ((0, 4),))
    tile_index = draw_tile_index(jax.random.fold_in(seeds[11], 71), 0)
    tile_values = bell_draw(seeds[6], (PARTITIONS * TILES, BLOCK, BLOCK), (3 * BLOCK) ** -0.5, 0.3125, ((0, 8),))
    tile_count = draw_tile_count(jax.random.fold_in(seeds[11], 71), 0)
    coupling = bell_draw(seeds[8], (PARTITIONS * HALO, NODES_DEV), HALO ** -0.5, 0.4375, ((0, 8),))
    bound_index = with_ends(jax.random.randint(seeds[9], (PARTITIONS, ROUNDS, BOUND_ROWS), 0, NODES_DEV), jax.random.fold_in(seeds[9], 1), 0, NODES_DEV - 1).astype(jnp.int32)
    bound_count = draw_bound_count(jax.random.fold_in(seeds[11], 71), 0)
    return dict(states_in=states_in, states_mid=states_mid, grad_out=grad_out, w_in=w_in, w_out=w_out, tile_index=tile_index, tile_values=tile_values, tile_count=tile_count, coupling=coupling, bound_index=bound_index, bound_count=bound_count)


def silu_grad(z):
    sig = jax.nn.sigmoid(z)
    return sig * (1.0 + z * (1.0 - sig))

def round_bit(r):
    levels = PARTITIONS.bit_length() - 1
    return r * (levels - 1) // (ROUNDS - 1)

def tiles_forward(x, index, values, count):
    blocks = NODES_DEV // BLOCK
    xb = x.reshape(blocks, BLOCK, D)

    def step(t, acc):
        prod = jnp.dot(values[t], xb[index[t, 1]], preferred_element_type=jnp.float32)
        prod = jnp.where(t < count, prod, jnp.zeros((), jnp.float32))
        return acc.at[index[t, 0]].add(prod)
    acc = lax.fori_loop(0, TILES, step, jnp.zeros((blocks, BLOCK, D), jnp.float32))
    return acc.reshape(NODES_DEV, D)

def tiles_backward(dm, index, values, count):
    blocks = NODES_DEV // BLOCK
    db = dm.reshape(blocks, BLOCK, D)

    def step(t, acc):
        prod = jnp.dot(values[t].T, db[index[t, 0]], preferred_element_type=jnp.float32)
        prod = jnp.where(t < count, prod, jnp.zeros((), jnp.float32))
        return acc.at[index[t, 1]].add(prod)
    acc = lax.fori_loop(0, TILES, step, jnp.zeros((blocks, BLOCK, D), jnp.float32))
    return acc.reshape(NODES_DEV, D)

def partner_of(r):
    owner = jnp.arange(PARTITIONS, dtype=jnp.int32)
    return jnp.bitwise_xor(owner, jnp.int32(1 << round_bit(r))).astype(jnp.int32)

def halo_all(x_all, bound_index, bound_count):
    slots = jnp.arange(BOUND_ROWS, dtype=jnp.int32)
    pieces = []
    for r in range(ROUNDS):
        other = partner_of(r)
        chosen = bound_index[other, r]
        rows = x_all[other[:, None], chosen]
        live = slots[None, :] < bound_count[other, r][:, None]
        pieces.append(jnp.where(live[..., None], rows, jnp.zeros((), x_all.dtype)))
    return jnp.concatenate(pieces, axis=1)

def returns_all(dg_all, bound_index, bound_count):
    slots = jnp.arange(BOUND_ROWS, dtype=jnp.int32)
    owner = jnp.arange(PARTITIONS, dtype=jnp.int32)
    total = jnp.zeros((PARTITIONS, NODES_DEV, D), jnp.float32)
    for r in range(ROUNDS):
        other = partner_of(r)
        incoming = dg_all[other, r * BOUND_ROWS:(r + 1) * BOUND_ROWS].astype(jnp.float32)
        live = slots[None, :] < bound_count[:, r][:, None]
        incoming = jnp.where(live[..., None], incoming, jnp.zeros((), jnp.float32))
        total = total.at[owner[:, None], bound_index[:, r]].add(incoming)
    return total

def layer_back(x_all, dout_all, weight_in, weight_out, index, values, count, couple, bound_index, bound_count):
    halo = halo_all(x_all, bound_index, bound_count)

    def aggregate(x, idx, vals, cnt, cpl, hal):
        part = tiles_forward(x, idx, vals, cnt)
        return (part + jnp.dot(cpl.T, hal, preferred_element_type=jnp.float32)).astype(jnp.bfloat16)
    merged = jax.vmap(aggregate)(x_all, index, values, count, couple, halo)
    flat_m = merged.reshape(PARTITIONS * NODES_DEV, D)
    flat_d = dout_all.reshape(PARTITIONS * NODES_DEV, D)
    z = jnp.dot(flat_m, weight_in, preferred_element_type=jnp.float32)
    ds = jnp.dot(flat_d, weight_out.T, preferred_element_type=jnp.float32)
    dz = (ds * silu_grad(z)).astype(jnp.bfloat16)
    dm = jnp.dot(dz, weight_in.T, preferred_element_type=jnp.float32).astype(jnp.bfloat16)
    dm = dm.reshape(PARTITIONS, NODES_DEV, D)

    def halo_grad(cpl, d):
        return jnp.dot(cpl, d, preferred_element_type=jnp.float32).astype(jnp.bfloat16)
    dg_all = jax.vmap(halo_grad)(couple, dm)
    inner = jax.vmap(tiles_backward)(dm, index, values, count)
    back = returns_all(dg_all, bound_index, bound_count)
    dx = dout_all.astype(jnp.float32) + inner + back
    return dx.astype(jnp.bfloat16)

def reference(states_in, states_mid, grad_out, w_in, w_out, tile_index, tile_values, tile_count, coupling, bound_index, bound_count):
    index = tile_index.reshape(PARTITIONS, TILES, 2)
    values = tile_values.reshape(PARTITIONS, TILES, BLOCK, BLOCK)
    couple = coupling.reshape(PARTITIONS, HALO, NODES_DEV)
    results = []
    for s in range(SECTIONS):
        x_mid = states_mid[s].reshape(PARTITIONS, NODES_DEV, D)
        x_in = states_in[s].reshape(PARTITIONS, NODES_DEV, D)
        dout = grad_out[s].reshape(PARTITIONS, NODES_DEV, D)
        dmid = layer_back(x_mid, dout, w_in[s, 1], w_out[s, 1], index, values, tile_count, couple, bound_index, bound_count)
        dfirst = layer_back(x_in, dmid, w_in[s, 0], w_out[s, 0], index, values, tile_count, couple, bound_index, bound_count)
        results.append(dfirst.reshape(NODES, D))
    shifted = results[1:] + [jnp.zeros((NODES, D), jnp.bfloat16)]
    return jnp.stack(shifted, axis=0)
```

```python
import functools

import jax
import jax.numpy as jnp
from jax import lax
from jax.experimental import pallas as pl
from jax.experimental.pallas import tpu as pltpu
from jax.sharding import PartitionSpec as P

MESH = pl.DeviceIdType.MESH
BF16 = jnp.bfloat16
F32 = jnp.float32
BLOCK = 128


def dot(a, b):
    return jnp.dot(a, b, preferred_element_type=F32)


def dot_t(a, b):
    return lax.dot_general(a, b, (((1,), (1,)), ((), ())), preferred_element_type=F32)


def silu_grad(z):
    half = 0.5 * jnp.tanh(0.5 * z)
    return (0.5 + half) + z * (0.25 - half * half)


def kernel(
    segments,
    bits,
    early,
    late,
    chunks,
    x_in_h,
    x_mid_h,
    dout_h,
    w_in_h,
    w_out_h,
    tile_index_h,
    tile_values_h,
    tile_count,
    coupling_h,
    bound_index_h,
    bound_count_h,
    out_h,
    tile_index,
    bound_count,
    bound_index,
    x_mid,
    x_in,
    dout,
    w_in,
    w_out,
    tiles,
    coup,
    adj,
    adj_t,
    coup_t,
    sel_t,
    sent,
    halo,
    dm,
    base,
    ds,
    zs,
    dg1,
    inc1,
    dg0,
    inc0,
    dxb,
    base_out,
    base_in,
    inc1_in,
    dm_in,
    late_in,
    dgx,
    incx,
    small_sem,
    load_sem,
    halo_send,
    halo_recv,
    g1_send,
    g1_recv,
    g0_send,
    g0_recv,
    gx_send,
    gx_recv,
    base_send,
    base_recv,
    inc_send,
    inc_recv,
    late_send,
    late_recv,
    out_send,
    out_recv,
):
    seg = lax.axis_index("segment")
    me = lax.axis_index("dom")
    nodes, width = x_mid.shape
    rounds = len(bits)
    rows = bound_index.shape[2]
    slots = tile_values_h.shape[0]
    blocks = nodes // BLOCK
    cw = width // chunks
    partners = []
    for bit in bits:
        mask = 1 << bit
        partners.append(me + mask - 2 * mask * lax.rem(me // mask, 2))
    order = list(range(rounds))[::-1]

    barrier = pltpu.get_barrier_semaphore()
    for r in order:
        pl.semaphore_signal(
            barrier, inc=1, device_id=(seg, partners[r]), device_id_type=MESH
        )

    @pl.when(seg > 0)
    def _():
        pl.semaphore_signal(barrier, inc=1, device_id=(seg - 1, me), device_id_type=MESH)

    @pl.when(seg < segments - 1)
    def _():
        pl.semaphore_signal(barrier, inc=1, device_id=(seg + 1, me), device_id_type=MESH)

    smalls = [
        pltpu.make_async_copy(src, dst, small_sem.at[i])
        for i, (src, dst) in enumerate(
            (
                (bound_index_h, bound_index),
                (bound_count_h, bound_count),
                (tile_index_h, tile_index),
            )
        )
    ]
    loads = [
        pltpu.make_async_copy(src, dst, load_sem.at[i])
        for i, (src, dst) in enumerate(
            (
                (x_mid_h.at[0], x_mid),
                (x_in_h.at[0], x_in),
                (tile_values_h, tiles.at[pl.ds(0, slots)]),
                (coupling_h, coup),
                (dout_h.at[0], dout),
                (w_out_h.at[0, 1], w_out.at[1]),
                (w_in_h.at[0, 1], w_in.at[1]),
                (w_in_h.at[0, 0], w_in.at[0]),
                (w_out_h.at[0, 0], w_out.at[0]),
            )
        )
    ]
    for small in smalls:
        small.start()
    for load in loads:
        load.start()

    def cols(c):
        return slice(c * cw, (c + 1) * cw)

    def piece(r):
        return pl.ds(r * rows, rows)

    for small in smalls:
        small.wait()
    picks = []
    for r in range(rounds):
        row = bound_index[r]
        lane = lax.broadcasted_iota(jnp.int32, (1, rows), 1)
        row = jnp.where(lane < bound_count[0, r], row, -1)
        sel_t[:, r * rows : (r + 1) * rows] = jnp.where(
            lax.broadcasted_iota(jnp.int32, (nodes, rows), 0) == row, 1.0, 0.0
        ).astype(BF16)
        square = lax.broadcasted_iota(jnp.int32, (rows, rows), 0) == lax.broadcasted_iota(
            jnp.int32, (rows, rows), 1
        )
        column = jnp.sum(jnp.where(square, row.astype(F32), 0.0), axis=1, keepdims=True)
        picks.append(
            jnp.where(
                lax.broadcasted_iota(jnp.int32, (rows, nodes), 1).astype(F32) == column, 1.0, 0.0
            ).astype(BF16)
        )
    sel = jnp.concatenate(picks, axis=0)

    loads[0].wait()
    sent[0] = dot(sel, x_mid[...]).astype(BF16)

    neighbours = jnp.minimum(seg, 1) + jnp.minimum(segments - 1 - seg, 1)
    pl.semaphore_wait(barrier, rounds + neighbours)

    def exchange(src, dst, r, send_sem, recv_sem):
        return pltpu.make_async_remote_copy(
            src_ref=src,
            dst_ref=dst,
            send_sem=send_sem,
            recv_sem=recv_sem,
            device_id=(seg, partners[r]),
            device_id_type=MESH,
        )

    def to_previous(src, dst, send_sem, recv_sem):
        return pltpu.make_async_remote_copy(
            src_ref=src,
            dst_ref=dst,
            send_sem=send_sem,
            recv_sem=recv_sem,
            device_id=(jnp.maximum(seg - 1, 0), me),
            device_id_type=MESH,
        )

    def grads(c, dg, inc, send_sem, recv_sem):
        return [
            exchange(
                dg.at[c, piece(r)], inc.at[c, piece(r)], r, send_sem.at[c, r], recv_sem.at[c, r]
            )
            for r in range(rounds)
        ]

    halos = [
        [
            exchange(
                sent.at[k, piece(r)], halo.at[k, piece(r)], r, halo_send.at[k, r], halo_recv.at[k, r]
            )
            for r in range(rounds)
        ]
        for k in range(2)
    ]
    copies1 = [grads(c, dg1, inc1, g1_send, g1_recv) for c in range(chunks)]
    copies0 = [grads(c, dg0, inc0, g0_send, g0_recv) for c in range(chunks - early)]
    copiesx = [grads(c, dgx, incx, gx_send, gx_recv) for c in range(early)]
    base_copy = to_previous(base_out, base_in, base_send.at[0], base_recv.at[0])
    inc_copies = [
        to_previous(inc1.at[c], inc1_in.at[c], inc_send.at[c], inc_recv.at[c]) for c in range(early)
    ]
    late_copies = [
        to_previous(inc0.at[c], late_in.at[c], late_send.at[c], late_recv.at[c]) for c in range(late)
    ]
    outs = [
        to_previous(
            dxb.at[c],
            dm_in.at[c] if c < early else out_h.at[0, :, pl.ds(c * cw, cw)],
            out_send.at[c],
            out_recv.at[c],
        )
        for c in range(chunks)
    ]

    def start_all(copies):
        for r in order:
            copies[r].start()

    def receive_all(copies):
        for r in order:
            copies[r].wait_recv()

    start_all(halos[0])
    loads[1].wait()
    sent[1] = dot(sel, x_in[...]).astype(BF16)

    tiles[slots] = jnp.zeros((BLOCK, BLOCK), BF16)
    loads[2].wait()
    keys = [
        jnp.where(t < tile_count[0], tile_index[0, t] * blocks + tile_index[1, t], -1)
        for t in range(slots)
    ]
    for a in range(blocks):
        for b in range(blocks):
            slot = jnp.int32(slots)
            for t in range(slots):
                slot = jnp.where(keys[t] == a * blocks + b, t, slot)
            tile = tiles[slot]
            adj[a * BLOCK : (a + 1) * BLOCK, b * BLOCK : (b + 1) * BLOCK] = tile
            adj_t[b * BLOCK : (b + 1) * BLOCK, a * BLOCK : (a + 1) * BLOCK] = tile.T
    loads[3].wait()
    coup_t[...] = coup[...].T

    merged = dot(adj[...], x_mid[...]).astype(BF16)
    loads[4].wait()
    loads[5].wait()
    ds[...] = dot_t(dout[...], w_out[1])
    loads[6].wait()
    zs[1] = dot(merged, w_in[1])
    merged = dot(adj[...], x_in[...]).astype(BF16)
    loads[7].wait()
    loads[8].wait()
    zs[0] = dot(merged, w_in[0])
    start_all(halos[1])

    receive_all(halos[0])
    far = dot(halo[0], w_in[1]).astype(BF16)
    z = zs[1] + dot(coup_t[...], far)
    dz = (ds[...] * silu_grad(z)).astype(BF16)

    for c in range(chunks):
        part = dot_t(dz, w_in[1, cols(c), :]).astype(BF16)
        dm[:, cols(c)] = part
        dg1[c] = dot(coup[...], part).astype(BF16)
        start_all(copies1[c])

    base[...] = dout[...].astype(F32) + dot(adj_t[...], dm[...])
    if early:
        base_out[...] = base[:, : early * cw].astype(BF16)

        @pl.when(seg > 0)
        def _():
            base_copy.start()

    ds[...] = dot_t(base[...].astype(BF16), w_out[0])
    receive_all(halos[1])
    far = dot(halo[1], w_in[0]).astype(BF16)
    zs[0] = silu_grad(zs[0] + dot(coup_t[...], far))
    far = None
    for c in range(chunks):
        receive_all(copies1[c])
        if c < early:

            @pl.when(seg > 0)
            def _():
                inc_copies[c].start()

        term = dot_t(inc1[c], w_out[0, :, cols(c)])
        far = term if far is None else far + term
    dz = ((ds[...] + dot(sel_t[...], far.astype(BF16))) * zs[0]).astype(BF16)

    def push(c):
        @pl.when(seg > 0)
        def _():
            outs[c].start()

    def without_far(c):
        got = (base[:, cols(c)] + dot(sel_t[...], inc1[c])).astype(BF16).astype(F32)
        return got + dot(adj_t[...], dm[:, cols(c)])

    for c in range(early):
        dxb[c] = dot_t(dz, w_in[0, cols(c), :]).astype(BF16)
        push(c)
    for c in range(early, chunks):
        part = dot_t(dz, w_in[0, cols(c), :]).astype(BF16)
        dm[:, cols(c)] = part
        dg0[c - early] = dot(coup[...], part).astype(BF16)
        start_all(copies0[c - early])
        if c < early + late:
            dxb[c] = without_far(c).astype(BF16)
            push(c)
    for c in range(early + late, chunks):
        base[:, cols(c)] = without_far(c)
    for c in range(early + late, chunks):
        receive_all(copies0[c - early])
        dxb[c] = (base[:, cols(c)] + dot(sel_t[...], inc0[c - early])).astype(BF16)
        push(c)
        if c == early + late:
            for k in range(late):
                receive_all(copies0[k])

                @pl.when(seg > 0)
                def _():
                    late_copies[k].start()

    @pl.when(seg == segments - 1)
    def _():
        out_h[...] = jnp.zeros(out_h.shape, BF16)

    @pl.when(seg < segments - 1)
    def _():
        for c in range(early):
            outs[c].wait_recv()
            dgx[c] = dot(coup[...], dm_in[c]).astype(BF16)
            start_all(copiesx[c])
            if c == 0:
                base_copy.wait_recv()
            inc_copies[c].wait_recv()
            got = base_in[:, cols(c)].astype(F32) + dot(sel_t[...], inc1_in[c])
            base[:, cols(c)] = got.astype(BF16).astype(F32) + dot(adj_t[...], dm_in[c])
        for c in range(early):
            receive_all(copiesx[c])
            out_h[0, :, cols(c)] = (base[:, cols(c)] + dot(sel_t[...], incx[c])).astype(BF16)
        for c in range(early):
            for copy in copiesx[c]:
                copy.wait_send()
        for c in range(late):
            late_copies[c].wait_recv()
            outs[early + c].wait_recv()
            got = out_h[0, :, cols(early + c)].astype(F32)
            out_h[0, :, cols(early + c)] = (got + dot(sel_t[...], late_in[c])).astype(BF16)
        for c in range(early + late, chunks):
            outs[c].wait_recv()

    for copies in halos + copies1 + copies0:
        for copy in copies:
            copy.wait_send()

    @pl.when(seg > 0)
    def _():
        if early:
            base_copy.wait_send()
        for copy in inc_copies + late_copies + outs:
            copy.wait_send()


def on_device(*args):
    (states_in, _, _, w_in, w_out, tile_index, tile_values, _, coupling, bound_index, _) = args
    args = args[:5] + (tile_index.T,) + args[6:9] + (bound_index.transpose(1, 0, 2), args[10])
    _, nodes, width = states_in.shape
    rounds, rows = bound_index.shape[1:]
    halo_rows = rounds * rows
    slots = tile_values.shape[0]
    segments = lax.axis_size("segment")
    levels = lax.axis_size("dom").bit_length() - 1
    bits = tuple(r * (levels - 1) // (rounds - 1) for r in range(rounds))
    early, late, chunks = 1, 0, 4
    cw = width // chunks
    whole = pl.BlockSpec(memory_space=pltpu.HBM)
    dma = pltpu.SemaphoreType.DMA
    args = tuple(
        a if i == 7 else pltpu.with_memory_space_constraint(a, pltpu.HBM) for i, a in enumerate(args)
    )
    return pl.pallas_call(
        functools.partial(kernel, segments, bits, early, late, chunks),
        out_shape=jax.ShapeDtypeStruct(states_in.shape, BF16),
        in_specs=[whole] * 7 + [pl.BlockSpec(memory_space=pltpu.SMEM)] + [whole] * 3,
        out_specs=pl.BlockSpec(memory_space=pltpu.VMEM),
        scratch_shapes=[
            pltpu.SMEM(args[5].shape, jnp.int32),
            pltpu.SMEM(args[10].shape, jnp.int32),
            pltpu.VMEM(args[9].shape, jnp.int32),
            pltpu.VMEM((nodes, width), BF16),
            pltpu.VMEM((nodes, width), BF16),
            pltpu.VMEM((nodes, width), BF16),
            pltpu.VMEM(w_in.shape[1:], BF16),
            pltpu.VMEM(w_out.shape[1:], BF16),
            pltpu.VMEM((slots + 1,) + tile_values.shape[1:], BF16),
            pltpu.VMEM((halo_rows, nodes), BF16),
            pltpu.VMEM((nodes, nodes), BF16),
            pltpu.VMEM((nodes, nodes), BF16),
            pltpu.VMEM((nodes, halo_rows), BF16),
            pltpu.VMEM((nodes, halo_rows), BF16),
            pltpu.VMEM((2, halo_rows, width), BF16),
            pltpu.VMEM((2, halo_rows, width), BF16),
            pltpu.VMEM((nodes, width), BF16),
            pltpu.VMEM((nodes, width), F32),
            pltpu.VMEM((nodes, width), F32),
            pltpu.VMEM((2, nodes, width), F32),
            pltpu.VMEM((chunks, halo_rows, cw), BF16),
            pltpu.VMEM((chunks, halo_rows, cw), BF16),
            pltpu.VMEM((chunks - early, halo_rows, cw), BF16),
            pltpu.VMEM((chunks - early, halo_rows, cw), BF16),
            pltpu.VMEM((chunks, nodes, cw), BF16),
            pltpu.VMEM((nodes, max(early, 1) * cw), BF16),
            pltpu.VMEM((nodes, max(early, 1) * cw), BF16),
            pltpu.VMEM((max(early, 1), halo_rows, cw), BF16),
            pltpu.VMEM((max(early, 1), nodes, cw), BF16),
            pltpu.VMEM((max(late, 1), halo_rows, cw), BF16),
            pltpu.VMEM((max(early, 1), halo_rows, cw), BF16),
            pltpu.VMEM((max(early, 1), halo_rows, cw), BF16),
            dma((3,)),
            dma((9,)),
            dma((2, rounds)),
            dma((2, rounds)),
            dma((chunks, rounds)),
            dma((chunks, rounds)),
            dma((chunks - early, rounds)),
            dma((chunks - early, rounds)),
            dma((max(early, 1), rounds)),
            dma((max(early, 1), rounds)),
            dma((1,)),
            dma((1,)),
            dma((max(early, 1),)),
            dma((max(early, 1),)),
            dma((max(late, 1),)),
            dma((max(late, 1),)),
            dma((chunks,)),
            dma((chunks,)),
        ],
        compiler_params=pltpu.CompilerParams(
            collective_id=0, has_side_effects=True, vmem_limit_bytes=32 * 2**20
        ),
    )(*args)


def solution(mesh):
    in_specs = (
        P("segment", "dom", None),
        P("segment", "dom", None),
        P("segment", "dom", None),
        P("segment", None, None, None),
        P("segment", None, None, None),
        P("dom", None),
        P("dom", None, None),
        P("dom"),
        P("dom", None),
        P("dom", None, None),
        P("dom", None),
    )
    out_specs = P("segment", "dom", None)
    return jax.shard_map(
        on_device, mesh=mesh, in_specs=in_specs, out_specs=out_specs, check_vma=False
    )
```

```python
import functools

import jax
import jax.numpy as jnp
from jax import lax
from jax.experimental import pallas as pl
from jax.experimental.pallas import tpu as pltpu
from jax.sharding import PartitionSpec as P

MESH = pl.DeviceIdType.MESH
BF16 = jnp.bfloat16
F32 = jnp.float32
BLOCK = 128


def dot(a, b):
    return jnp.dot(a, b, preferred_element_type=F32)


def dot_t(a, b):
    return lax.dot_general(a, b, (((1,), (1,)), ((), ())), preferred_element_type=F32)


def silu_grad(z):
    half = 0.5 * jnp.tanh(0.5 * z)
    return (0.5 + half) + z * (0.25 - half * half)


def kernel(
    segments,
    bits,
    early,
    late,
    chunks,
    x_in_h,
    x_mid_h,
    dout_h,
    w_in_h,
    w_out_h,
    tile_index_h,
    tile_values_h,
    tile_count,
    coupling_h,
    bound_index_h,
    bound_count_h,
    out_h,
    tile_index,
    bound_count,
    bound_index,
    x_mid,
    x_in,
    dout,
    w_in,
    w_out,
    tiles,
    coup,
    adj,
    adj_t,
    coup_t,
    sel_t,
    sent,
    halo,
    dm,
    base,
    ds,
    zs,
    dg1,
    inc1,
    dg0,
    inc0,
    dxb,
    base_out,
    base_in,
    dg1_in,
    dm_in,
    late_in,
    dgx,
    incx,
    small_sem,
    load_sem,
    halo_send,
    halo_recv,
    g1_send,
    g1_recv,
    g0_send,
    g0_recv,
    gx_send,
    gx_recv,
    base_send,
    base_recv,
    dg_send,
    dg_recv,
    late_send,
    late_recv,
    out_send,
    out_recv,
):
    seg = lax.axis_index("segment")
    me = lax.axis_index("dom")
    nodes, width = x_mid.shape
    rounds = len(bits)
    rows = bound_index.shape[2]
    slots = tile_values_h.shape[0]
    blocks = nodes // BLOCK
    cw = width // chunks
    partners = []
    for bit in bits:
        mask = 1 << bit
        partners.append(me + mask - 2 * mask * lax.rem(me // mask, 2))
    order = list(range(rounds))[::-1]

    barrier = pltpu.get_barrier_semaphore()
    for r in order:
        pl.semaphore_signal(
            barrier, inc=1, device_id=(seg, partners[r]), device_id_type=MESH
        )

    @pl.when(seg > 0)
    def _():
        pl.semaphore_signal(barrier, inc=1, device_id=(seg - 1, me), device_id_type=MESH)

    @pl.when(seg < segments - 1)
    def _():
        pl.semaphore_signal(barrier, inc=1, device_id=(seg + 1, me), device_id_type=MESH)

    smalls = [
        pltpu.make_async_copy(src, dst, small_sem.at[i])
        for i, (src, dst) in enumerate(
            (
                (bound_index_h, bound_index),
                (bound_count_h, bound_count),
                (tile_index_h, tile_index),
            )
        )
    ]
    loads = [
        pltpu.make_async_copy(src, dst, load_sem.at[i])
        for i, (src, dst) in enumerate(
            (
                (x_mid_h.at[0], x_mid),
                (x_in_h.at[0], x_in),
                (tile_values_h, tiles.at[pl.ds(0, slots)]),
                (coupling_h, coup),
                (dout_h.at[0], dout),
                (w_out_h.at[0, 1], w_out.at[1]),
                (w_in_h.at[0, 1], w_in.at[1]),
                (w_in_h.at[0, 0], w_in.at[0]),
                (w_out_h.at[0, 0], w_out.at[0]),
            )
        )
    ]
    for small in smalls:
        small.start()
    for load in loads:
        load.start()

    def cols(c):
        return slice(c * cw, (c + 1) * cw)

    def piece(r):
        return pl.ds(r * rows, rows)

    for small in smalls:
        small.wait()
    places = []
    picks = []
    for r in range(rounds):
        row = bound_index[r]
        lane = lax.broadcasted_iota(jnp.int32, (1, rows), 1)
        row = jnp.where(lane < bound_count[0, r], row, -1)
        places.append(row)
        square = lax.broadcasted_iota(jnp.int32, (rows, rows), 0) == lax.broadcasted_iota(
            jnp.int32, (rows, rows), 1
        )
        column = jnp.sum(jnp.where(square, row.astype(F32), 0.0), axis=1, keepdims=True)
        picks.append(
            jnp.where(
                lax.broadcasted_iota(jnp.int32, (rows, nodes), 1).astype(F32) == column, 1.0, 0.0
            ).astype(BF16)
        )
    sel = jnp.concatenate(picks, axis=0)

    loads[0].wait()
    sent[0] = dot(sel, x_mid[...]).astype(BF16)

    neighbours = jnp.minimum(seg, 1) + jnp.minimum(segments - 1 - seg, 1)
    pl.semaphore_wait(barrier, rounds + neighbours)

    def exchange(src, dst, r, send_sem, recv_sem):
        return pltpu.make_async_remote_copy(
            src_ref=src,
            dst_ref=dst,
            send_sem=send_sem,
            recv_sem=recv_sem,
            device_id=(seg, partners[r]),
            device_id_type=MESH,
        )

    def to_previous(src, dst, send_sem, recv_sem):
        return pltpu.make_async_remote_copy(
            src_ref=src,
            dst_ref=dst,
            send_sem=send_sem,
            recv_sem=recv_sem,
            device_id=(jnp.maximum(seg - 1, 0), me),
            device_id_type=MESH,
        )

    def grads(c, dg, inc, send_sem, recv_sem):
        return [
            exchange(
                dg.at[c, piece(r)], inc.at[c, piece(r)], r, send_sem.at[c, r], recv_sem.at[c, r]
            )
            for r in range(rounds)
        ]

    halos = [
        [
            exchange(
                sent.at[k, piece(r)], halo.at[k, piece(r)], r, halo_send.at[k, r], halo_recv.at[k, r]
            )
            for r in range(rounds)
        ]
        for k in range(2)
    ]
    copies1 = [grads(c, dg1, inc1, g1_send, g1_recv) for c in range(chunks)]
    copies0 = [grads(c, dg0, inc0, g0_send, g0_recv) for c in range(chunks - early)]
    copiesx = [grads(c, dgx, incx, gx_send, gx_recv) for c in range(early)]
    base_copy = to_previous(base_out, base_in, base_send.at[0], base_recv.at[0])
    dg_copies = [
        to_previous(dg1.at[c], dg1_in.at[c], dg_send.at[c], dg_recv.at[c]) for c in range(early)
    ]
    late_copies = [
        to_previous(inc0.at[c], late_in.at[c], late_send.at[c], late_recv.at[c]) for c in range(late)
    ]
    outs = [
        to_previous(
            dxb.at[c],
            dm_in.at[c] if c < early else out_h.at[0, :, pl.ds(c * cw, cw)],
            out_send.at[c],
            out_recv.at[c],
        )
        for c in range(chunks)
    ]

    def start_all(copies):
        for r in order:
            copies[r].start()

    def receive_all(copies):
        for r in order:
            copies[r].wait_recv()

    start_all(halos[0])
    for r in range(rounds):
        sel_t[:, r * rows : (r + 1) * rows] = jnp.where(
            lax.broadcasted_iota(jnp.int32, (nodes, rows), 0) == places[r], 1.0, 0.0
        ).astype(BF16)
    loads[1].wait()
    sent[1] = dot(sel, x_in[...]).astype(BF16)

    tiles[slots] = jnp.zeros((BLOCK, BLOCK), BF16)
    loads[2].wait()
    keys = [
        jnp.where(t < tile_count[0], tile_index[0, t] * blocks + tile_index[1, t], -1)
        for t in range(slots)
    ]
    for a in range(blocks):
        for b in range(blocks):
            slot = jnp.int32(slots)
            for t in range(slots):
                slot = jnp.where(keys[t] == a * blocks + b, t, slot)
            tile = tiles[slot]
            adj[a * BLOCK : (a + 1) * BLOCK, b * BLOCK : (b + 1) * BLOCK] = tile
            adj_t[b * BLOCK : (b + 1) * BLOCK, a * BLOCK : (a + 1) * BLOCK] = tile.T
    loads[3].wait()
    coup_t[...] = coup[...].T

    merged = dot(adj[...], x_mid[...]).astype(BF16)
    loads[4].wait()
    loads[5].wait()
    ds[...] = dot_t(dout[...], w_out[1])
    loads[6].wait()
    zs[1] = dot(merged, w_in[1])
    merged = dot(adj[...], x_in[...]).astype(BF16)
    loads[7].wait()
    loads[8].wait()
    zs[0] = dot(merged, w_in[0])
    start_all(halos[1])

    receive_all(halos[0])
    far = dot(halo[0], w_in[1]).astype(BF16)
    z = zs[1] + dot(coup_t[...], far)
    dz = (ds[...] * silu_grad(z)).astype(BF16)

    for c in range(chunks):
        part = dot_t(dz, w_in[1, cols(c), :]).astype(BF16)
        dm[:, cols(c)] = part
        dg1[c] = dot(coup[...], part).astype(BF16)
        start_all(copies1[c])
        if c < early:

            @pl.when(seg > 0)
            def _():
                dg_copies[c].start()

    base[...] = dout[...].astype(F32) + dot(adj_t[...], dm[...])
    if early:
        base_out[...] = base[:, : early * cw].astype(BF16)

        @pl.when(seg > 0)
        def _():
            base_copy.start()

    ds[...] = dot_t(base[...].astype(BF16), w_out[0])
    receive_all(halos[1])
    far = dot(halo[1], w_in[0]).astype(BF16)
    zs[0] = silu_grad(zs[0] + dot(coup_t[...], far))
    far = None
    for c in range(chunks):
        receive_all(copies1[c])
        term = dot_t(inc1[c], w_out[0, :, cols(c)])
        far = term if far is None else far + term
    dz = ((ds[...] + dot(sel_t[...], far.astype(BF16))) * zs[0]).astype(BF16)

    def push(c):
        @pl.when(seg > 0)
        def _():
            outs[c].start()

    def without_far(c):
        got = (base[:, cols(c)] + dot(sel_t[...], inc1[c])).astype(BF16).astype(F32)
        return got + dot(adj_t[...], dm[:, cols(c)])

    for c in range(early):
        dxb[c] = dot_t(dz, w_in[0, cols(c), :]).astype(BF16)
        push(c)
    for c in range(early, chunks):
        part = dot_t(dz, w_in[0, cols(c), :]).astype(BF16)
        dm[:, cols(c)] = part
        dg0[c - early] = dot(coup[...], part).astype(BF16)
        start_all(copies0[c - early])
        if c < early + late:
            dxb[c] = without_far(c).astype(BF16)
            push(c)
    for c in range(early + late, chunks):
        base[:, cols(c)] = without_far(c)
    for c in range(early + late, chunks):
        receive_all(copies0[c - early])
        dxb[c] = (base[:, cols(c)] + dot(sel_t[...], inc0[c - early])).astype(BF16)
        push(c)
        if c == early + late:
            for k in range(late):
                receive_all(copies0[k])

                @pl.when(seg > 0)
                def _():
                    late_copies[k].start()

    @pl.when(seg == segments - 1)
    def _():
        out_h[...] = jnp.zeros(out_h.shape, BF16)

    @pl.when(seg < segments - 1)
    def _():
        for c in range(early):
            outs[c].wait_recv()
            dg_copies[c].wait_recv()
            dgx[c] = (dg1_in[c].astype(F32) + dot(coup[...], dm_in[c])).astype(BF16)
            start_all(copiesx[c])
            if c == 0:
                base_copy.wait_recv()
            base[:, cols(c)] = base_in[:, cols(c)].astype(F32) + dot(adj_t[...], dm_in[c])
        for c in range(early):
            receive_all(copiesx[c])
            out_h[0, :, cols(c)] = (base[:, cols(c)] + dot(sel_t[...], incx[c])).astype(BF16)
        for c in range(early):
            for copy in copiesx[c]:
                copy.wait_send()
        for c in range(late):
            late_copies[c].wait_recv()
            outs[early + c].wait_recv()
            got = out_h[0, :, cols(early + c)].astype(F32)
            out_h[0, :, cols(early + c)] = (got + dot(sel_t[...], late_in[c])).astype(BF16)
        for c in range(early + late, chunks):
            outs[c].wait_recv()

    for copies in halos + copies1 + copies0:
        for copy in copies:
            copy.wait_send()

    @pl.when(seg > 0)
    def _():
        if early:
            base_copy.wait_send()
        for copy in dg_copies + late_copies + outs:
            copy.wait_send()


def on_device(*args):
    (states_in, _, _, w_in, w_out, tile_index, tile_values, _, coupling, bound_index, _) = args
    args = args[:5] + (tile_index.T,) + args[6:9] + (bound_index.transpose(1, 0, 2), args[10])
    _, nodes, width = states_in.shape
    rounds, rows = bound_index.shape[1:]
    halo_rows = rounds * rows
    slots = tile_values.shape[0]
    segments = lax.axis_size("segment")
    levels = lax.axis_size("dom").bit_length() - 1
    bits = tuple(r * (levels - 1) // (rounds - 1) for r in range(rounds))
    early, late, chunks = 1, 0, 4
    cw = width // chunks
    whole = pl.BlockSpec(memory_space=pltpu.HBM)
    dma = pltpu.SemaphoreType.DMA
    args = tuple(
        a if i == 7 else pltpu.with_memory_space_constraint(a, pltpu.HBM) for i, a in enumerate(args)
    )
    return pl.pallas_call(
        functools.partial(kernel, segments, bits, early, late, chunks),
        out_shape=jax.ShapeDtypeStruct(states_in.shape, BF16),
        in_specs=[whole] * 7 + [pl.BlockSpec(memory_space=pltpu.SMEM)] + [whole] * 3,
        out_specs=pl.BlockSpec(memory_space=pltpu.VMEM),
        scratch_shapes=[
            pltpu.SMEM(args[5].shape, jnp.int32),
            pltpu.SMEM(args[10].shape, jnp.int32),
            pltpu.VMEM(args[9].shape, jnp.int32),
            pltpu.VMEM((nodes, width), BF16),
            pltpu.VMEM((nodes, width), BF16),
            pltpu.VMEM((nodes, width), BF16),
            pltpu.VMEM(w_in.shape[1:], BF16),
            pltpu.VMEM(w_out.shape[1:], BF16),
            pltpu.VMEM((slots + 1,) + tile_values.shape[1:], BF16),
            pltpu.VMEM((halo_rows, nodes), BF16),
            pltpu.VMEM((nodes, nodes), BF16),
            pltpu.VMEM((nodes, nodes), BF16),
            pltpu.VMEM((nodes, halo_rows), BF16),
            pltpu.VMEM((nodes, halo_rows), BF16),
            pltpu.VMEM((2, halo_rows, width), BF16),
            pltpu.VMEM((2, halo_rows, width), BF16),
            pltpu.VMEM((nodes, width), BF16),
            pltpu.VMEM((nodes, width), F32),
            pltpu.VMEM((nodes, width), F32),
            pltpu.VMEM((2, nodes, width), F32),
            pltpu.VMEM((chunks, halo_rows, cw), BF16),
            pltpu.VMEM((chunks, halo_rows, cw), BF16),
            pltpu.VMEM((chunks - early, halo_rows, cw), BF16),
            pltpu.VMEM((chunks - early, halo_rows, cw), BF16),
            pltpu.VMEM((chunks, nodes, cw), BF16),
            pltpu.VMEM((nodes, max(early, 1) * cw), BF16),
            pltpu.VMEM((nodes, max(early, 1) * cw), BF16),
            pltpu.VMEM((max(early, 1), halo_rows, cw), BF16),
            pltpu.VMEM((max(early, 1), nodes, cw), BF16),
            pltpu.VMEM((max(late, 1), halo_rows, cw), BF16),
            pltpu.VMEM((max(early, 1), halo_rows, cw), BF16),
            pltpu.VMEM((max(early, 1), halo_rows, cw), BF16),
            dma((3,)),
            dma((9,)),
            dma((2, rounds)),
            dma((2, rounds)),
            dma((chunks, rounds)),
            dma((chunks, rounds)),
            dma((chunks - early, rounds)),
            dma((chunks - early, rounds)),
            dma((max(early, 1), rounds)),
            dma((max(early, 1), rounds)),
            dma((1,)),
            dma((1,)),
            dma((max(early, 1),)),
            dma((max(early, 1),)),
            dma((max(late, 1),)),
            dma((max(late, 1),)),
            dma((chunks,)),
            dma((chunks,)),
        ],
        compiler_params=pltpu.CompilerParams(
            collective_id=0, has_side_effects=True, vmem_limit_bytes=32 * 2**20
        ),
    )(*args)


def solution(mesh):
    in_specs = (
        P("segment", "dom", None),
        P("segment", "dom", None),
        P("segment", "dom", None),
        P("segment", None, None, None),
        P("segment", None, None, None),
        P("dom", None),
        P("dom", None, None),
        P("dom"),
        P("dom", None),
        P("dom", None, None),
        P("dom", None),
    )
    out_specs = P("segment", "dom", None)
    return jax.shard_map(
        on_device, mesh=mesh, in_specs=in_specs, out_specs=out_specs, check_vma=False
    )
```

```python
import functools

import jax
import jax.numpy as jnp
from jax import lax
from jax.experimental import pallas as pl
from jax.experimental.pallas import tpu as pltpu
from jax.sharding import PartitionSpec as P

MESH = pl.DeviceIdType.MESH
BF16 = jnp.bfloat16
F32 = jnp.float32
BLOCK = 128


def dot(a, b):
    return jnp.dot(a, b, preferred_element_type=F32)


def dot_t(a, b):
    return lax.dot_general(a, b, (((1,), (1,)), ((), ())), preferred_element_type=F32)


def silu_grad(z):
    half = 0.5 * jnp.tanh(0.5 * z)
    return (0.5 + half) + z * (0.25 - half * half)


def kernel(
    segments,
    bits,
    early,
    chunks,
    held,
    gate,
    x_in_h,
    x_mid_h,
    dout_h,
    w_in_h,
    w_out_h,
    tile_index_h,
    tile_values_h,
    tile_count,
    coupling_h,
    bound_index_h,
    bound_count_h,
    out_h,
    tile_index,
    bound_count,
    bound_index,
    x_mid,
    x_in,
    dout,
    w_in,
    w_out,
    tiles,
    coup,
    adj,
    adj_t,
    coup_t,
    sel_t,
    sent,
    halo,
    dm,
    base,
    ds,
    zs,
    dg1,
    inc1,
    dg0,
    inc0,
    dxb,
    base_out,
    base_in,
    dg1_in,
    dm_in,
    dgx,
    incx,
    small_sem,
    load_sem,
    halo_send,
    halo_recv,
    g1_send,
    g1_recv,
    g0_send,
    g0_recv,
    gx_send,
    gx_recv,
    base_send,
    base_recv,
    dg_send,
    dg_recv,
    out_send,
    out_recv,
    turn,
):
    seg = lax.axis_index("segment")
    me = lax.axis_index("dom")
    core = lax.rem(me, 2)
    nodes, width = x_mid.shape
    rounds = len(bits)
    rows = bound_index.shape[2]
    slots = tile_values_h.shape[0]
    blocks = nodes // BLOCK
    cw = width // chunks
    partners = []
    for bit in bits:
        mask = 1 << bit
        partners.append(me + mask - 2 * mask * lax.rem(me // mask, 2))
    order = list(range(rounds))[::-1]

    barrier = pltpu.get_barrier_semaphore()
    for r in order:
        pl.semaphore_signal(
            barrier, inc=1, device_id=(seg, partners[r]), device_id_type=MESH
        )

    @pl.when(seg > 0)
    def _():
        pl.semaphore_signal(barrier, inc=1, device_id=(seg - 1, me), device_id_type=MESH)

    @pl.when(seg < segments - 1)
    def _():
        pl.semaphore_signal(barrier, inc=1, device_id=(seg + 1, me), device_id_type=MESH)

    smalls = [
        pltpu.make_async_copy(src, dst, small_sem.at[i])
        for i, (src, dst) in enumerate(
            (
                (bound_index_h, bound_index),
                (bound_count_h, bound_count),
                (tile_index_h, tile_index),
            )
        )
    ]
    loads = [
        pltpu.make_async_copy(src, dst, load_sem.at[i])
        for i, (src, dst) in enumerate(
            (
                (x_mid_h.at[0], x_mid),
                (x_in_h.at[0], x_in),
                (tile_values_h, tiles.at[pl.ds(0, slots)]),
                (coupling_h, coup),
                (dout_h.at[0], dout),
                (w_out_h.at[0, 1], w_out.at[1]),
                (w_in_h.at[0, 1], w_in.at[1]),
                (w_in_h.at[0, 0], w_in.at[0]),
                (w_out_h.at[0, 0], w_out.at[0]),
            )
        )
    ]
    for small in smalls:
        small.start()
    for load in loads:
        load.start()

    def cols(c):
        return slice(c * cw, (c + 1) * cw)

    def piece(r):
        return pl.ds(r * rows, rows)

    for small in smalls:
        small.wait()
    places = []
    picks = []
    for r in range(rounds):
        row = bound_index[r]
        lane = lax.broadcasted_iota(jnp.int32, (1, rows), 1)
        row = jnp.where(lane < bound_count[0, r], row, -1)
        places.append(row)
        square = lax.broadcasted_iota(jnp.int32, (rows, rows), 0) == lax.broadcasted_iota(
            jnp.int32, (rows, rows), 1
        )
        column = jnp.sum(jnp.where(square, row.astype(F32), 0.0), axis=1, keepdims=True)
        picks.append(
            jnp.where(
                lax.broadcasted_iota(jnp.int32, (rows, nodes), 1).astype(F32) == column, 1.0, 0.0
            ).astype(BF16)
        )
    sel = jnp.concatenate(picks, axis=0)

    loads[0].wait()
    sent[0] = dot(sel, x_mid[...]).astype(BF16)

    neighbours = jnp.minimum(seg, 1) + jnp.minimum(segments - 1 - seg, 1)
    pl.semaphore_wait(barrier, rounds + neighbours)

    def exchange(src, dst, r, send_sem, recv_sem):
        return pltpu.make_async_remote_copy(
            src_ref=src,
            dst_ref=dst,
            send_sem=send_sem,
            recv_sem=recv_sem,
            device_id=(seg, partners[r]),
            device_id_type=MESH,
        )

    def to_previous(src, dst, send_sem, recv_sem):
        return pltpu.make_async_remote_copy(
            src_ref=src,
            dst_ref=dst,
            send_sem=send_sem,
            recv_sem=recv_sem,
            device_id=(jnp.maximum(seg - 1, 0), me),
            device_id_type=MESH,
        )

    def grads(c, dg, inc, send_sem, recv_sem):
        return [
            exchange(
                dg.at[c, piece(r)], inc.at[c, piece(r)], r, send_sem.at[c, r], recv_sem.at[c, r]
            )
            for r in range(rounds)
        ]

    halos = [
        [
            exchange(
                sent.at[k, piece(r)], halo.at[k, piece(r)], r, halo_send.at[k, r], halo_recv.at[k, r]
            )
            for r in range(rounds)
        ]
        for k in range(2)
    ]
    copies1 = [grads(c, dg1, inc1, g1_send, g1_recv) for c in range(chunks)]
    copies0 = [grads(c, dg0, inc0, g0_send, g0_recv) for c in range(chunks - early)]
    copiesx = [grads(c, dgx, incx, gx_send, gx_recv) for c in range(early)]
    base_copy = to_previous(base_out, base_in, base_send.at[0], base_recv.at[0])
    dg_copies = [
        to_previous(dg1.at[c], dg1_in.at[c], dg_send.at[c], dg_recv.at[c]) for c in range(early)
    ]
    outs = [
        to_previous(
            dxb.at[c],
            dm_in.at[c] if c < early else out_h.at[0, :, pl.ds(c * cw, cw)],
            out_send.at[c],
            out_recv.at[c],
        )
        for c in range(chunks)
    ]

    def start_all(copies):
        for r in order:
            copies[r].start()

    def receive_all(copies):
        for r in order:
            copies[r].wait_recv()

    start_all(halos[0])
    for r in range(rounds):
        sel_t[:, r * rows : (r + 1) * rows] = jnp.where(
            lax.broadcasted_iota(jnp.int32, (nodes, rows), 0) == places[r], 1.0, 0.0
        ).astype(BF16)
    loads[1].wait()
    sent[1] = dot(sel, x_in[...]).astype(BF16)

    tiles[slots] = jnp.zeros((BLOCK, BLOCK), BF16)
    loads[2].wait()
    keys = [
        jnp.where(t < tile_count[0], tile_index[0, t] * blocks + tile_index[1, t], -1)
        for t in range(slots)
    ]
    for a in range(blocks):
        for b in range(blocks):
            slot = jnp.int32(slots)
            for t in range(slots):
                slot = jnp.where(keys[t] == a * blocks + b, t, slot)
            tile = tiles[slot]
            adj[a * BLOCK : (a + 1) * BLOCK, b * BLOCK : (b + 1) * BLOCK] = tile
            adj_t[b * BLOCK : (b + 1) * BLOCK, a * BLOCK : (a + 1) * BLOCK] = tile.T
    loads[3].wait()
    coup_t[...] = coup[...].T

    merged = dot(adj[...], x_mid[...]).astype(BF16)
    loads[4].wait()
    loads[5].wait()
    ds[...] = dot_t(dout[...], w_out[1])
    loads[6].wait()
    zs[1] = dot(merged, w_in[1])
    merged = dot(adj[...], x_in[...]).astype(BF16)
    loads[7].wait()
    loads[8].wait()
    zs[0] = dot(merged, w_in[0])
    start_all(halos[1])

    receive_all(halos[0])
    far = dot(halo[0], w_in[1]).astype(BF16)
    z = zs[1] + dot(coup_t[...], far)
    dz = (ds[...] * silu_grad(z)).astype(BF16)

    for c in range(chunks):
        part = dot_t(dz, w_in[1, cols(c), :]).astype(BF16)
        dm[:, cols(c)] = part
        dg1[c] = dot(coup[...], part).astype(BF16)
        start_all(copies1[c])
        if c < early:

            @pl.when(seg > 0)
            def _():
                dg_copies[c].start()

    base[...] = dout[...].astype(F32) + dot(adj_t[...], dm[...])
    base_out[...] = base[:, : early * cw].astype(BF16)

    @pl.when(seg > 0)
    def _():
        base_copy.start()

    ds[...] = dot_t(base[...].astype(BF16), w_out[0])
    receive_all(halos[1])
    far = dot(halo[1], w_in[0]).astype(BF16)
    zs[0] = silu_grad(zs[0] + dot(coup_t[...], far))
    far = None
    for c in range(chunks):
        receive_all(copies1[c])
        term = dot_t(inc1[c], w_out[0, :, cols(c)])
        far = term if far is None else far + term
    dz = ((ds[...] + dot(sel_t[...], far.astype(BF16))) * zs[0]).astype(BF16)

    def push(c):
        @pl.when(seg > 0)
        def _():
            outs[c].start()

    def without_far(c):
        got = (base[:, cols(c)] + dot(sel_t[...], inc1[c])).astype(BF16).astype(F32)
        return got + dot(adj_t[...], dm[:, cols(c)])

    for c in range(early):
        dxb[c] = dot_t(dz, w_in[0, cols(c), :]).astype(BF16)
        push(c)
    for c in range(early, chunks):
        part = dot_t(dz, w_in[0, cols(c), :]).astype(BF16)
        dm[:, cols(c)] = part
        dg0[c - early] = dot(coup[...], part).astype(BF16)
        start_all(copies0[c - early])
        if c < early:
            dxb[c] = without_far(c).astype(BF16)
            push(c)
    for c in range(early, chunks):
        base[:, cols(c)] = without_far(c)
    for c in range(early, chunks):
        receive_all(copies0[c - early])
        dxb[c] = (base[:, cols(c)] + dot(sel_t[...], inc0[c - early])).astype(BF16)

        @pl.when((seg > 0) & ((core == 0) | (c < chunks - held)))
        def _():
            outs[c].start()

    @pl.when(seg == segments - 1)
    def _():
        out_h[...] = jnp.zeros(out_h.shape, BF16)

    @pl.when(seg < segments - 1)
    def _():
        for c in range(early):
            outs[c].wait_recv()
            dg_copies[c].wait_recv()
            dgx[c] = (dg1_in[c].astype(F32) + dot(coup[...], dm_in[c])).astype(BF16)
            start_all(copiesx[c])
            if c == 0:
                base_copy.wait_recv()
            base[:, cols(c)] = base_in[:, cols(c)].astype(F32) + dot(adj_t[...], dm_in[c])

    @pl.when((seg > 0) & (core == 0))
    def _():
        for c in range(gate + 1):
            outs[c].wait_send()
        pl.semaphore_signal(turn, inc=1, device_id=(seg, partners[0]), device_id_type=MESH)

    @pl.when((seg > 0) & (core > 0))
    def _():
        pl.semaphore_wait(turn, 1)
        for c in range(chunks - held, chunks):
            outs[c].start()

    @pl.when(seg < segments - 1)
    def _():
        for c in range(early):
            receive_all(copiesx[c])
            out_h[0, :, cols(c)] = (base[:, cols(c)] + dot(sel_t[...], incx[c])).astype(BF16)
        for c in range(early):
            for copy in copiesx[c]:
                copy.wait_send()
        for c in range(early, chunks):
            outs[c].wait_recv()

    for copies in halos + copies1 + copies0:
        for copy in copies:
            copy.wait_send()

    @pl.when(seg > 0)
    def _():
        base_copy.wait_send()
        for copy in dg_copies + outs[gate + 1 :]:
            copy.wait_send()

    @pl.when((seg > 0) & (core > 0))
    def _():
        for copy in outs[: gate + 1]:
            copy.wait_send()


def on_device(*args):
    (states_in, _, _, w_in, w_out, tile_index, tile_values, _, coupling, bound_index, _) = args
    args = args[:5] + (tile_index.T,) + args[6:9] + (bound_index.transpose(1, 0, 2), args[10])
    _, nodes, width = states_in.shape
    rounds, rows = bound_index.shape[1:]
    halo_rows = rounds * rows
    slots = tile_values.shape[0]
    segments = lax.axis_size("segment")
    levels = lax.axis_size("dom").bit_length() - 1
    bits = tuple(r * (levels - 1) // (rounds - 1) for r in range(rounds))
    early, chunks, held, gate = 1, 4, 1, 2
    cw = width // chunks
    whole = pl.BlockSpec(memory_space=pltpu.HBM)
    dma = pltpu.SemaphoreType.DMA
    args = tuple(
        a if i == 7 else pltpu.with_memory_space_constraint(a, pltpu.HBM) for i, a in enumerate(args)
    )
    return pl.pallas_call(
        functools.partial(kernel, segments, bits, early, chunks, held, gate),
        out_shape=jax.ShapeDtypeStruct(states_in.shape, BF16),
        in_specs=[whole] * 7 + [pl.BlockSpec(memory_space=pltpu.SMEM)] + [whole] * 3,
        out_specs=pl.BlockSpec(memory_space=pltpu.VMEM),
        scratch_shapes=[
            pltpu.SMEM(args[5].shape, jnp.int32),
            pltpu.SMEM(args[10].shape, jnp.int32),
            pltpu.VMEM(args[9].shape, jnp.int32),
            pltpu.VMEM((nodes, width), BF16),
            pltpu.VMEM((nodes, width), BF16),
            pltpu.VMEM((nodes, width), BF16),
            pltpu.VMEM(w_in.shape[1:], BF16),
            pltpu.VMEM(w_out.shape[1:], BF16),
            pltpu.VMEM((slots + 1,) + tile_values.shape[1:], BF16),
            pltpu.VMEM((halo_rows, nodes), BF16),
            pltpu.VMEM((nodes, nodes), BF16),
            pltpu.VMEM((nodes, nodes), BF16),
            pltpu.VMEM((nodes, halo_rows), BF16),
            pltpu.VMEM((nodes, halo_rows), BF16),
            pltpu.VMEM((2, halo_rows, width), BF16),
            pltpu.VMEM((2, halo_rows, width), BF16),
            pltpu.VMEM((nodes, width), BF16),
            pltpu.VMEM((nodes, width), F32),
            pltpu.VMEM((nodes, width), F32),
            pltpu.VMEM((2, nodes, width), F32),
            pltpu.VMEM((chunks, halo_rows, cw), BF16),
            pltpu.VMEM((chunks, halo_rows, cw), BF16),
            pltpu.VMEM((chunks - early, halo_rows, cw), BF16),
            pltpu.VMEM((chunks - early, halo_rows, cw), BF16),
            pltpu.VMEM((chunks, nodes, cw), BF16),
            pltpu.VMEM((nodes, early * cw), BF16),
            pltpu.VMEM((nodes, early * cw), BF16),
            pltpu.VMEM((early, halo_rows, cw), BF16),
            pltpu.VMEM((early, nodes, cw), BF16),
            pltpu.VMEM((early, halo_rows, cw), BF16),
            pltpu.VMEM((early, halo_rows, cw), BF16),
            dma((3,)),
            dma((9,)),
            dma((2, rounds)),
            dma((2, rounds)),
            dma((chunks, rounds)),
            dma((chunks, rounds)),
            dma((chunks - early, rounds)),
            dma((chunks - early, rounds)),
            dma((early, rounds)),
            dma((early, rounds)),
            dma((1,)),
            dma((1,)),
            dma((early,)),
            dma((early,)),
            dma((chunks,)),
            dma((chunks,)),
            pltpu.SemaphoreType.REGULAR,
        ],
        compiler_params=pltpu.CompilerParams(
            collective_id=0, has_side_effects=True, vmem_limit_bytes=32 * 2**20
        ),
    )(*args)


def solution(mesh):
    in_specs = (
        P("segment", "dom", None),
        P("segment", "dom", None),
        P("segment", "dom", None),
        P("segment", None, None, None),
        P("segment", None, None, None),
        P("dom", None),
        P("dom", None, None),
        P("dom"),
        P("dom", None),
        P("dom", None, None),
        P("dom", None),
    )
    out_specs = P("segment", "dom", None)
    return jax.shard_map(
        on_device, mesh=mesh, in_specs=in_specs, out_specs=out_specs, check_vma=False
    )
```

```python
import functools

import jax
import jax.numpy as jnp
from jax import lax
from jax.experimental import pallas as pl
from jax.experimental.pallas import tpu as pltpu
from jax.sharding import PartitionSpec as P

MESH = pl.DeviceIdType.MESH
BF16 = jnp.bfloat16
F32 = jnp.float32
BLOCK = 128


def dot(a, b):
    return jnp.dot(a, b, preferred_element_type=F32)


def dot_t(a, b):
    return lax.dot_general(a, b, (((1,), (1,)), ((), ())), preferred_element_type=F32)


def silu_grad(z):
    half = 0.5 * jnp.tanh(0.5 * z)
    return (0.5 + half) + z * (0.25 - half * half)


def kernel(
    segments,
    bits,
    early,
    chunks,
    held,
    gate,
    x_in_h,
    x_mid_h,
    dout_h,
    w_in_h,
    w_out_h,
    tile_index_h,
    tile_values_h,
    tile_count,
    coupling_h,
    bound_index_h,
    bound_count_h,
    out_h,
    tile_index,
    bound_count,
    bound_index,
    x_mid,
    x_in,
    dout,
    w_in,
    w_out,
    tiles,
    coup,
    adj,
    adj_t,
    coup_t,
    sel_t,
    sent,
    halo,
    dm,
    base,
    ds,
    zs,
    dg1,
    inc1,
    dg0,
    inc0,
    dxb,
    base_out,
    base_in,
    dg1_in,
    dm_in,
    dgx,
    incx,
    small_sem,
    load_sem,
    halo_send,
    halo_recv,
    g1_send,
    g1_recv,
    g0_send,
    g0_recv,
    gx_send,
    gx_recv,
    base_send,
    base_recv,
    dg_send,
    dg_recv,
    out_send,
    out_recv,
    turn,
):
    seg = lax.axis_index("segment")
    me = lax.axis_index("dom")
    core = lax.rem(me, 2)
    nodes, width = x_mid.shape
    rounds = len(bits)
    rows = bound_index.shape[2]
    slots = tile_values_h.shape[0]
    blocks = nodes // BLOCK
    cw = width // chunks
    partners = []
    for bit in bits:
        mask = 1 << bit
        partners.append(me + mask - 2 * mask * lax.rem(me // mask, 2))
    order = list(range(rounds))[::-1]

    barrier = pltpu.get_barrier_semaphore()
    for r in order:
        pl.semaphore_signal(
            barrier, inc=1, device_id=(seg, partners[r]), device_id_type=MESH
        )

    @pl.when(seg > 0)
    def _():
        pl.semaphore_signal(barrier, inc=1, device_id=(seg - 1, me), device_id_type=MESH)

    @pl.when(seg < segments - 1)
    def _():
        pl.semaphore_signal(barrier, inc=1, device_id=(seg + 1, me), device_id_type=MESH)

    smalls = [
        pltpu.make_async_copy(src, dst, small_sem.at[i])
        for i, (src, dst) in enumerate(
            (
                (bound_index_h, bound_index),
                (bound_count_h, bound_count),
                (tile_index_h, tile_index),
            )
        )
    ]
    loads = [
        pltpu.make_async_copy(src, dst, load_sem.at[i])
        for i, (src, dst) in enumerate(
            (
                (x_mid_h.at[0], x_mid),
                (x_in_h.at[0], x_in),
                (tile_values_h, tiles.at[pl.ds(0, slots)]),
                (coupling_h, coup),
                (dout_h.at[0], dout),
                (w_out_h.at[0, 1], w_out.at[1]),
                (w_in_h.at[0, 1], w_in.at[1]),
                (w_in_h.at[0, 0], w_in.at[0]),
                (w_out_h.at[0, 0], w_out.at[0]),
            )
        )
    ]
    for small in smalls:
        small.start()
    loads[0].start()

    def cols(c):
        return slice(c * cw, (c + 1) * cw)

    def piece(r):
        return pl.ds(r * rows, rows)

    for small in smalls:
        small.wait()
    places = []
    picks = []
    for r in range(rounds):
        row = bound_index[r]
        lane = lax.broadcasted_iota(jnp.int32, (1, rows), 1)
        row = jnp.where(lane < bound_count[0, r], row, -1)
        places.append(row)
        square = lax.broadcasted_iota(jnp.int32, (rows, rows), 0) == lax.broadcasted_iota(
            jnp.int32, (rows, rows), 1
        )
        column = jnp.sum(jnp.where(square, row.astype(F32), 0.0), axis=1, keepdims=True)
        picks.append(
            jnp.where(
                lax.broadcasted_iota(jnp.int32, (rows, nodes), 1).astype(F32) == column, 1.0, 0.0
            ).astype(BF16)
        )
    sel = jnp.concatenate(picks, axis=0)
    for load in loads[1:]:
        load.start()

    loads[0].wait()
    sent[0] = dot(sel, x_mid[...]).astype(BF16)

    neighbours = jnp.minimum(seg, 1) + jnp.minimum(segments - 1 - seg, 1)
    pl.semaphore_wait(barrier, rounds + neighbours)

    def exchange(src, dst, r, send_sem, recv_sem):
        return pltpu.make_async_remote_copy(
            src_ref=src,
            dst_ref=dst,
            send_sem=send_sem,
            recv_sem=recv_sem,
            device_id=(seg, partners[r]),
            device_id_type=MESH,
        )

    def to_previous(src, dst, send_sem, recv_sem):
        return pltpu.make_async_remote_copy(
            src_ref=src,
            dst_ref=dst,
            send_sem=send_sem,
            recv_sem=recv_sem,
            device_id=(jnp.maximum(seg - 1, 0), me),
            device_id_type=MESH,
        )

    def grads(c, dg, inc, send_sem, recv_sem):
        return [
            exchange(
                dg.at[c, piece(r)], inc.at[c, piece(r)], r, send_sem.at[c, r], recv_sem.at[c, r]
            )
            for r in range(rounds)
        ]

    halos = [
        [
            exchange(
                sent.at[k, piece(r)], halo.at[k, piece(r)], r, halo_send.at[k, r], halo_recv.at[k, r]
            )
            for r in range(rounds)
        ]
        for k in range(2)
    ]
    copies1 = [grads(c, dg1, inc1, g1_send, g1_recv) for c in range(chunks)]
    copies0 = [grads(c, dg0, inc0, g0_send, g0_recv) for c in range(chunks - early)]
    copiesx = [grads(c, dgx, incx, gx_send, gx_recv) for c in range(early)]
    base_copy = to_previous(base_out, base_in, base_send.at[0], base_recv.at[0])
    dg_copies = [
        to_previous(dg1.at[c], dg1_in.at[c], dg_send.at[c], dg_recv.at[c]) for c in range(early)
    ]
    outs = [
        to_previous(
            dxb.at[c],
            dm_in.at[c] if c < early else out_h.at[0, :, pl.ds(c * cw, cw)],
            out_send.at[c],
            out_recv.at[c],
        )
        for c in range(chunks)
    ]

    def start_all(copies):
        for r in order:
            copies[r].start()

    def receive_all(copies):
        for r in order:
            copies[r].wait_recv()

    start_all(halos[0])
    for r in range(rounds):
        sel_t[:, r * rows : (r + 1) * rows] = jnp.where(
            lax.broadcasted_iota(jnp.int32, (nodes, rows), 0) == places[r], 1.0, 0.0
        ).astype(BF16)
    loads[1].wait()
    sent[1] = dot(sel, x_in[...]).astype(BF16)

    tiles[slots] = jnp.zeros((BLOCK, BLOCK), BF16)
    loads[2].wait()
    keys = [
        jnp.where(t < tile_count[0], tile_index[0, t] * blocks + tile_index[1, t], -1)
        for t in range(slots)
    ]
    for a in range(blocks):
        for b in range(blocks):
            slot = jnp.int32(slots)
            for t in range(slots):
                slot = jnp.where(keys[t] == a * blocks + b, t, slot)
            tile = tiles[slot]
            adj[a * BLOCK : (a + 1) * BLOCK, b * BLOCK : (b + 1) * BLOCK] = tile
            adj_t[b * BLOCK : (b + 1) * BLOCK, a * BLOCK : (a + 1) * BLOCK] = tile.T
    loads[3].wait()
    coup_t[...] = coup[...].T

    merged = dot(adj[...], x_mid[...]).astype(BF16)
    loads[4].wait()
    loads[5].wait()
    ds[...] = dot_t(dout[...], w_out[1])
    loads[6].wait()
    zs[1] = dot(merged, w_in[1])
    merged = dot(adj[...], x_in[...]).astype(BF16)
    loads[7].wait()
    loads[8].wait()
    zs[0] = dot(merged, w_in[0])
    start_all(halos[1])

    receive_all(halos[0])
    far = dot(halo[0], w_in[1]).astype(BF16)
    z = zs[1] + dot(coup_t[...], far)
    dz = (ds[...] * silu_grad(z)).astype(BF16)

    for c in range(chunks):
        part = dot_t(dz, w_in[1, cols(c), :]).astype(BF16)
        dm[:, cols(c)] = part
        dg1[c] = dot(coup[...], part).astype(BF16)
        start_all(copies1[c])
        if c < early:

            @pl.when(seg > 0)
            def _():
                dg_copies[c].start()

    base[...] = dout[...].astype(F32) + dot(adj_t[...], dm[...])
    base_out[...] = base[:, : early * cw].astype(BF16)

    @pl.when(seg > 0)
    def _():
        base_copy.start()

    ds[...] = dot_t(base[...].astype(BF16), w_out[0])
    receive_all(halos[1])
    far = dot(halo[1], w_in[0]).astype(BF16)
    zs[0] = silu_grad(zs[0] + dot(coup_t[...], far))
    far = None
    for c in range(chunks):
        receive_all(copies1[c])
        term = dot_t(inc1[c], w_out[0, :, cols(c)])
        far = term if far is None else far + term
    dz = ((ds[...] + dot(sel_t[...], far.astype(BF16))) * zs[0]).astype(BF16)

    def push(c):
        @pl.when(seg > 0)
        def _():
            outs[c].start()

    def without_far(c):
        got = (base[:, cols(c)] + dot(sel_t[...], inc1[c])).astype(BF16).astype(F32)
        return got + dot(adj_t[...], dm[:, cols(c)])

    for c in range(early):
        dxb[c] = dot_t(dz, w_in[0, cols(c), :]).astype(BF16)
        push(c)
    for c in range(early, chunks):
        part = dot_t(dz, w_in[0, cols(c), :]).astype(BF16)
        dm[:, cols(c)] = part
        dg0[c - early] = dot(coup[...], part).astype(BF16)
        start_all(copies0[c - early])
        if c < early:
            dxb[c] = without_far(c).astype(BF16)
            push(c)
    for c in range(early, chunks):
        base[:, cols(c)] = without_far(c)
    for c in range(early, chunks):
        receive_all(copies0[c - early])
        dxb[c] = (base[:, cols(c)] + dot(sel_t[...], inc0[c - early])).astype(BF16)

        @pl.when((seg > 0) & ((core == 0) | (c < chunks - held)))
        def _():
            outs[c].start()

    @pl.when(seg == segments - 1)
    def _():
        out_h[...] = jnp.zeros(out_h.shape, BF16)

    @pl.when(seg < segments - 1)
    def _():
        for c in range(early):
            outs[c].wait_recv()
            dg_copies[c].wait_recv()
            dgx[c] = (dg1_in[c].astype(F32) + dot(coup[...], dm_in[c])).astype(BF16)
            start_all(copiesx[c])
            if c == 0:
                base_copy.wait_recv()
            base[:, cols(c)] = base_in[:, cols(c)].astype(F32) + dot(adj_t[...], dm_in[c])

    @pl.when((seg > 0) & (core == 0))
    def _():
        for c in range(gate + 1):
            outs[c].wait_send()
        pl.semaphore_signal(turn, inc=1, device_id=(seg, partners[0]), device_id_type=MESH)

    @pl.when((seg > 0) & (core > 0))
    def _():
        pl.semaphore_wait(turn, 1)
        for c in range(chunks - held, chunks):
            outs[c].start()

    @pl.when(seg < segments - 1)
    def _():
        for c in range(early):
            receive_all(copiesx[c])
            out_h[0, :, cols(c)] = (base[:, cols(c)] + dot(sel_t[...], incx[c])).astype(BF16)
        for c in range(early):
            for copy in copiesx[c]:
                copy.wait_send()
        for c in range(early, chunks):
            outs[c].wait_recv()

    for copies in halos + copies1 + copies0:
        for copy in copies:
            copy.wait_send()

    @pl.when(seg > 0)
    def _():
        base_copy.wait_send()
        for copy in dg_copies + outs[gate + 1 :]:
            copy.wait_send()

    @pl.when((seg > 0) & (core > 0))
    def _():
        for copy in outs[: gate + 1]:
            copy.wait_send()


def on_device(*args):
    (states_in, _, _, w_in, w_out, tile_index, tile_values, _, coupling, bound_index, _) = args
    args = args[:5] + (tile_index.T,) + args[6:9] + (bound_index.transpose(1, 0, 2), args[10])
    _, nodes, width = states_in.shape
    rounds, rows = bound_index.shape[1:]
    halo_rows = rounds * rows
    slots = tile_values.shape[0]
    segments = lax.axis_size("segment")
    levels = lax.axis_size("dom").bit_length() - 1
    bits = tuple(r * (levels - 1) // (rounds - 1) for r in range(rounds))
    early, chunks, held, gate = 1, 4, 1, 2
    cw = width // chunks
    whole = pl.BlockSpec(memory_space=pltpu.HBM)
    dma = pltpu.SemaphoreType.DMA
    args = tuple(
        a if i == 7 else pltpu.with_memory_space_constraint(a, pltpu.HBM) for i, a in enumerate(args)
    )
    return pl.pallas_call(
        functools.partial(kernel, segments, bits, early, chunks, held, gate),
        out_shape=jax.ShapeDtypeStruct(states_in.shape, BF16),
        in_specs=[whole] * 7 + [pl.BlockSpec(memory_space=pltpu.SMEM)] + [whole] * 3,
        out_specs=pl.BlockSpec(memory_space=pltpu.VMEM),
        scratch_shapes=[
            pltpu.SMEM(args[5].shape, jnp.int32),
            pltpu.SMEM(args[10].shape, jnp.int32),
            pltpu.VMEM(args[9].shape, jnp.int32),
            pltpu.VMEM((nodes, width), BF16),
            pltpu.VMEM((nodes, width), BF16),
            pltpu.VMEM((nodes, width), BF16),
            pltpu.VMEM(w_in.shape[1:], BF16),
            pltpu.VMEM(w_out.shape[1:], BF16),
            pltpu.VMEM((slots + 1,) + tile_values.shape[1:], BF16),
            pltpu.VMEM((halo_rows, nodes), BF16),
            pltpu.VMEM((nodes, nodes), BF16),
            pltpu.VMEM((nodes, nodes), BF16),
            pltpu.VMEM((nodes, halo_rows), BF16),
            pltpu.VMEM((nodes, halo_rows), BF16),
            pltpu.VMEM((2, halo_rows, width), BF16),
            pltpu.VMEM((2, halo_rows, width), BF16),
            pltpu.VMEM((nodes, width), BF16),
            pltpu.VMEM((nodes, width), F32),
            pltpu.VMEM((nodes, width), F32),
            pltpu.VMEM((2, nodes, width), F32),
            pltpu.VMEM((chunks, halo_rows, cw), BF16),
            pltpu.VMEM((chunks, halo_rows, cw), BF16),
            pltpu.VMEM((chunks - early, halo_rows, cw), BF16),
            pltpu.VMEM((chunks - early, halo_rows, cw), BF16),
            pltpu.VMEM((chunks, nodes, cw), BF16),
            pltpu.VMEM((nodes, early * cw), BF16),
            pltpu.VMEM((nodes, early * cw), BF16),
            pltpu.VMEM((early, halo_rows, cw), BF16),
            pltpu.VMEM((early, nodes, cw), BF16),
            pltpu.VMEM((early, halo_rows, cw), BF16),
            pltpu.VMEM((early, halo_rows, cw), BF16),
            dma((3,)),
            dma((9,)),
            dma((2, rounds)),
            dma((2, rounds)),
            dma((chunks, rounds)),
            dma((chunks, rounds)),
            dma((chunks - early, rounds)),
            dma((chunks - early, rounds)),
            dma((early, rounds)),
            dma((early, rounds)),
            dma((1,)),
            dma((1,)),
            dma((early,)),
            dma((early,)),
            dma((chunks,)),
            dma((chunks,)),
            pltpu.SemaphoreType.REGULAR,
        ],
        compiler_params=pltpu.CompilerParams(
            collective_id=0, has_side_effects=True, vmem_limit_bytes=32 * 2**20
        ),
    )(*args)


def solution(mesh):
    in_specs = (
        P("segment", "dom", None),
        P("segment", "dom", None),
        P("segment", "dom", None),
        P("segment", None, None, None),
        P("segment", None, None, None),
        P("dom", None),
        P("dom", None, None),
        P("dom"),
        P("dom", None),
        P("dom", None, None),
        P("dom", None),
    )
    out_specs = P("segment", "dom", None)
    return jax.shard_map(
        on_device, mesh=mesh, in_specs=in_specs, out_specs=out_specs, check_vma=False
    )
```

```python
import functools

import jax
import jax.numpy as jnp
from jax import lax
from jax.experimental import pallas as pl
from jax.experimental.pallas import tpu as pltpu
from jax.sharding import PartitionSpec as P

MESH = pl.DeviceIdType.MESH
BF16 = jnp.bfloat16
F32 = jnp.float32
BLOCK = 128


def dot(a, b):
    return jnp.dot(a, b, preferred_element_type=F32)


def dot_t(a, b):
    return lax.dot_general(a, b, (((1,), (1,)), ((), ())), preferred_element_type=F32)


def silu_grad(z):
    half = 0.5 * jnp.tanh(0.5 * z)
    return (0.5 + half) + z * (0.25 - half * half)


def kernel(
    segments,
    bits,
    early,
    chunks,
    held,
    gate,
    x_in_h,
    x_mid_h,
    dout_h,
    w_in_h,
    w_out_h,
    tile_index_h,
    tile_values_h,
    tile_count,
    coupling_h,
    bound_index_h,
    bound_count_h,
    out_h,
    tile_index,
    bound_count,
    bound_index,
    x_mid,
    x_in,
    dout,
    w_in,
    w_out,
    tiles,
    coup,
    adj,
    adj_t,
    coup_t,
    sel_t,
    sent,
    halo,
    dm,
    base,
    ds,
    zs,
    dg1,
    inc1,
    dg0,
    inc0,
    dxb,
    base_out,
    base_in,
    dg1_in,
    dm_in,
    dgx,
    incx,
    small_sem,
    load_sem,
    halo_send,
    halo_recv,
    g1_send,
    g1_recv,
    g0_send,
    g0_recv,
    gx_send,
    gx_recv,
    base_send,
    base_recv,
    dg_send,
    dg_recv,
    out_send,
    out_recv,
    turn,
):
    seg = lax.axis_index("segment")
    me = lax.axis_index("dom")
    core = lax.rem(me, 2)
    nodes, width = x_mid.shape
    rounds = len(bits)
    rows = bound_index.shape[2]
    slots = tile_values_h.shape[0]
    blocks = nodes // BLOCK
    cw = width // chunks
    partners = []
    for bit in bits:
        mask = 1 << bit
        partners.append(me + mask - 2 * mask * lax.rem(me // mask, 2))
    order = list(range(rounds))[::-1]

    barrier = pltpu.get_barrier_semaphore()
    for r in order:
        pl.semaphore_signal(
            barrier, inc=1, device_id=(seg, partners[r]), device_id_type=MESH
        )

    @pl.when(seg > 0)
    def _():
        pl.semaphore_signal(barrier, inc=1, device_id=(seg - 1, me), device_id_type=MESH)

    @pl.when(seg < segments - 1)
    def _():
        pl.semaphore_signal(barrier, inc=1, device_id=(seg + 1, me), device_id_type=MESH)

    smalls = [
        pltpu.make_async_copy(src, dst, small_sem.at[i])
        for i, (src, dst) in enumerate(
            (
                (bound_index_h, bound_index),
                (bound_count_h, bound_count),
                (tile_index_h, tile_index),
            )
        )
    ]
    loads = [
        pltpu.make_async_copy(src, dst, load_sem.at[i])
        for i, (src, dst) in enumerate(
            (
                (x_mid_h.at[0], x_mid),
                (x_in_h.at[0], x_in),
                (tile_values_h, tiles.at[pl.ds(0, slots)]),
                (coupling_h, coup),
                (dout_h.at[0], dout),
                (w_out_h.at[0, 1], w_out.at[1]),
                (w_in_h.at[0, 1], w_in.at[1]),
                (w_in_h.at[0, 0], w_in.at[0]),
                (w_out_h.at[0, 0], w_out.at[0]),
            )
        )
    ]
    for small in smalls:
        small.start()
    loads[0].start()

    def cols(c):
        return slice(c * cw, (c + 1) * cw)

    def piece(r):
        return pl.ds(r * rows, rows)

    for small in smalls:
        small.wait()
    places = []
    picks = []
    for r in range(rounds):
        row = bound_index[r]
        lane = lax.broadcasted_iota(jnp.int32, (1, rows), 1)
        row = jnp.where(lane < bound_count[0, r], row, -1)
        places.append(row)
        square = lax.broadcasted_iota(jnp.int32, (rows, rows), 0) == lax.broadcasted_iota(
            jnp.int32, (rows, rows), 1
        )
        column = jnp.sum(jnp.where(square, row.astype(F32), 0.0), axis=1, keepdims=True)
        picks.append(
            jnp.where(
                lax.broadcasted_iota(jnp.int32, (rows, nodes), 1).astype(F32) == column, 1.0, 0.0
            ).astype(BF16)
        )
    sel = jnp.concatenate(picks, axis=0)
    for load in loads[1:]:
        load.start()

    loads[0].wait()
    sent[0] = dot(sel, x_mid[...]).astype(BF16)

    neighbours = jnp.minimum(seg, 1) + jnp.minimum(segments - 1 - seg, 1)
    pl.semaphore_wait(barrier, rounds + neighbours)

    def exchange(src, dst, r, send_sem, recv_sem):
        return pltpu.make_async_remote_copy(
            src_ref=src,
            dst_ref=dst,
            send_sem=send_sem,
            recv_sem=recv_sem,
            device_id=(seg, partners[r]),
            device_id_type=MESH,
        )

    def to_previous(src, dst, send_sem, recv_sem):
        return pltpu.make_async_remote_copy(
            src_ref=src,
            dst_ref=dst,
            send_sem=send_sem,
            recv_sem=recv_sem,
            device_id=(jnp.maximum(seg - 1, 0), me),
            device_id_type=MESH,
        )

    def grads(c, dg, inc, send_sem, recv_sem):
        return [
            exchange(
                dg.at[c, piece(r)], inc.at[c, piece(r)], r, send_sem.at[c, r], recv_sem.at[c, r]
            )
            for r in range(rounds)
        ]

    halos = [
        [
            exchange(
                sent.at[k, piece(r)], halo.at[k, piece(r)], r, halo_send.at[k, r], halo_recv.at[k, r]
            )
            for r in range(rounds)
        ]
        for k in range(2)
    ]
    copies1 = [grads(c, dg1, inc1, g1_send, g1_recv) for c in range(chunks)]
    copies0 = [grads(c, dg0, inc0, g0_send, g0_recv) for c in range(chunks - early)]
    copiesx = [grads(c, dgx, incx, gx_send, gx_recv) for c in range(early)]
    base_copy = to_previous(base_out, base_in, base_send.at[0], base_recv.at[0])
    dg_copies = [
        to_previous(dg1.at[c], dg1_in.at[c], dg_send.at[c], dg_recv.at[c]) for c in range(early)
    ]
    outs = [
        to_previous(
            dxb.at[c],
            dm_in.at[c] if c < early else out_h.at[0, :, pl.ds(c * cw, cw)],
            out_send.at[c],
            out_recv.at[c],
        )
        for c in range(chunks)
    ]

    def start_all(copies):
        for r in order:
            copies[r].start()

    def receive_all(copies):
        for r in order:
            copies[r].wait_recv()

    start_all(halos[0])
    for r in range(rounds):
        sel_t[:, r * rows : (r + 1) * rows] = jnp.where(
            lax.broadcasted_iota(jnp.int32, (nodes, rows), 0) == places[r], 1.0, 0.0
        ).astype(BF16)
    loads[1].wait()
    sent[1] = dot(sel, x_in[...]).astype(BF16)

    tiles[slots] = jnp.zeros((BLOCK, BLOCK), BF16)
    loads[2].wait()
    keys = [
        jnp.where(t < tile_count[0], tile_index[0, t] * blocks + tile_index[1, t], -1)
        for t in range(slots)
    ]
    for a in range(blocks):
        for b in range(blocks):
            slot = jnp.int32(slots)
            for t in range(slots):
                slot = jnp.where(keys[t] == a * blocks + b, t, slot)
            tile = tiles[slot]
            adj[a * BLOCK : (a + 1) * BLOCK, b * BLOCK : (b + 1) * BLOCK] = tile
            adj_t[b * BLOCK : (b + 1) * BLOCK, a * BLOCK : (a + 1) * BLOCK] = tile.T
    loads[3].wait()
    coup_t[...] = coup[...].T

    merged = dot(adj[...], x_mid[...]).astype(BF16)
    loads[4].wait()
    loads[5].wait()
    ds[...] = dot_t(dout[...], w_out[1])
    loads[6].wait()
    zs[1] = dot(merged, w_in[1])
    merged = dot(adj[...], x_in[...]).astype(BF16)
    loads[7].wait()
    loads[8].wait()
    zs[0] = dot(merged, w_in[0])
    start_all(halos[1])

    receive_all(halos[0])
    far = dot(halo[0], w_in[1]).astype(BF16)
    z = zs[1] + dot(coup_t[...], far)
    dz = (ds[...] * silu_grad(z)).astype(BF16)

    for c in range(chunks):
        if c % 2 == 0:
            wide = dot_t(dz, w_in[1, c * cw : (c + 2) * cw, :]).astype(BF16)
            dm[:, c * cw : (c + 2) * cw] = wide
            grad = dot(coup[...], wide).astype(BF16)
        dg1[c] = grad[:, (c % 2) * cw : (c % 2 + 1) * cw]
        start_all(copies1[c])
        if c < early:

            @pl.when(seg > 0)
            def _():
                dg_copies[c].start()

    base[...] = dout[...].astype(F32) + dot(adj_t[...], dm[...])
    base_out[...] = base[:, : early * cw].astype(BF16)

    @pl.when(seg > 0)
    def _():
        base_copy.start()

    ds[...] = dot_t(base[...].astype(BF16), w_out[0])
    receive_all(halos[1])
    far = dot(halo[1], w_in[0]).astype(BF16)
    zs[0] = silu_grad(zs[0] + dot(coup_t[...], far))
    far = None
    for c in range(chunks):
        receive_all(copies1[c])
        term = dot_t(inc1[c], w_out[0, :, cols(c)])
        far = term if far is None else far + term
    dz = ((ds[...] + dot(sel_t[...], far.astype(BF16))) * zs[0]).astype(BF16)

    def push(c):
        @pl.when(seg > 0)
        def _():
            outs[c].start()

    def without_far(c):
        got = (base[:, cols(c)] + dot(sel_t[...], inc1[c])).astype(BF16).astype(F32)
        return got + dot(adj_t[...], dm[:, cols(c)])

    for c in range(early):
        dxb[c] = dot_t(dz, w_in[0, cols(c), :]).astype(BF16)
        push(c)
    for c in range(early, chunks):
        part = dot_t(dz, w_in[0, cols(c), :]).astype(BF16)
        dm[:, cols(c)] = part
        dg0[c - early] = dot(coup[...], part).astype(BF16)
        start_all(copies0[c - early])
        if c < early:
            dxb[c] = without_far(c).astype(BF16)
            push(c)
    for c in range(early, chunks):
        base[:, cols(c)] = without_far(c)
    for c in range(early, chunks):
        receive_all(copies0[c - early])
        dxb[c] = (base[:, cols(c)] + dot(sel_t[...], inc0[c - early])).astype(BF16)

        @pl.when((seg > 0) & ((core == 0) | (c < chunks - held)))
        def _():
            outs[c].start()

    @pl.when(seg == segments - 1)
    def _():
        out_h[...] = jnp.zeros(out_h.shape, BF16)

    @pl.when(seg < segments - 1)
    def _():
        for c in range(early):
            outs[c].wait_recv()
            dg_copies[c].wait_recv()
            dgx[c] = (dg1_in[c].astype(F32) + dot(coup[...], dm_in[c])).astype(BF16)
            start_all(copiesx[c])
            if c == 0:
                base_copy.wait_recv()
            base[:, cols(c)] = base_in[:, cols(c)].astype(F32) + dot(adj_t[...], dm_in[c])

    @pl.when((seg > 0) & (core == 0))
    def _():
        for c in range(gate + 1):
            outs[c].wait_send()
        pl.semaphore_signal(turn, inc=1, device_id=(seg, partners[0]), device_id_type=MESH)

    @pl.when((seg > 0) & (core > 0))
    def _():
        pl.semaphore_wait(turn, 1)
        for c in range(chunks - held, chunks):
            outs[c].start()

    @pl.when(seg < segments - 1)
    def _():
        for c in range(early):
            receive_all(copiesx[c])
            out_h[0, :, cols(c)] = (base[:, cols(c)] + dot(sel_t[...], incx[c])).astype(BF16)
        for c in range(early):
            for copy in copiesx[c]:
                copy.wait_send()
        for c in range(early, chunks):
            outs[c].wait_recv()

    for copies in halos + copies1 + copies0:
        for copy in copies:
            copy.wait_send()

    @pl.when(seg > 0)
    def _():
        base_copy.wait_send()
        for copy in dg_copies + outs[gate + 1 :]:
            copy.wait_send()

    @pl.when((seg > 0) & (core > 0))
    def _():
        for copy in outs[: gate + 1]:
            copy.wait_send()


def on_device(*args):
    (states_in, _, _, w_in, w_out, tile_index, tile_values, _, coupling, bound_index, _) = args
    args = args[:5] + (tile_index.T,) + args[6:9] + (bound_index.transpose(1, 0, 2), args[10])
    _, nodes, width = states_in.shape
    rounds, rows = bound_index.shape[1:]
    halo_rows = rounds * rows
    slots = tile_values.shape[0]
    segments = lax.axis_size("segment")
    levels = lax.axis_size("dom").bit_length() - 1
    bits = tuple(r * (levels - 1) // (rounds - 1) for r in range(rounds))
    early, chunks, held, gate = 1, 4, 1, 2
    cw = width // chunks
    whole = pl.BlockSpec(memory_space=pltpu.HBM)
    dma = pltpu.SemaphoreType.DMA
    args = tuple(
        a if i == 7 else pltpu.with_memory_space_constraint(a, pltpu.HBM) for i, a in enumerate(args)
    )
    return pl.pallas_call(
        functools.partial(kernel, segments, bits, early, chunks, held, gate),
        out_shape=jax.ShapeDtypeStruct(states_in.shape, BF16),
        in_specs=[whole] * 7 + [pl.BlockSpec(memory_space=pltpu.SMEM)] + [whole] * 3,
        out_specs=pl.BlockSpec(memory_space=pltpu.VMEM),
        scratch_shapes=[
            pltpu.SMEM(args[5].shape, jnp.int32),
            pltpu.SMEM(args[10].shape, jnp.int32),
            pltpu.VMEM(args[9].shape, jnp.int32),
            pltpu.VMEM((nodes, width), BF16),
            pltpu.VMEM((nodes, width), BF16),
            pltpu.VMEM((nodes, width), BF16),
            pltpu.VMEM(w_in.shape[1:], BF16),
            pltpu.VMEM(w_out.shape[1:], BF16),
            pltpu.VMEM((slots + 1,) + tile_values.shape[1:], BF16),
            pltpu.VMEM((halo_rows, nodes), BF16),
            pltpu.VMEM((nodes, nodes), BF16),
            pltpu.VMEM((nodes, nodes), BF16),
            pltpu.VMEM((nodes, halo_rows), BF16),
            pltpu.VMEM((nodes, halo_rows), BF16),
            pltpu.VMEM((2, halo_rows, width), BF16),
            pltpu.VMEM((2, halo_rows, width), BF16),
            pltpu.VMEM((nodes, width), BF16),
            pltpu.VMEM((nodes, width), F32),
            pltpu.VMEM((nodes, width), F32),
            pltpu.VMEM((2, nodes, width), F32),
            pltpu.VMEM((chunks, halo_rows, cw), BF16),
            pltpu.VMEM((chunks, halo_rows, cw), BF16),
            pltpu.VMEM((chunks - early, halo_rows, cw), BF16),
            pltpu.VMEM((chunks - early, halo_rows, cw), BF16),
            pltpu.VMEM((chunks, nodes, cw), BF16),
            pltpu.VMEM((nodes, early * cw), BF16),
            pltpu.VMEM((nodes, early * cw), BF16),
            pltpu.VMEM((early, halo_rows, cw), BF16),
            pltpu.VMEM((early, nodes, cw), BF16),
            pltpu.VMEM((early, halo_rows, cw), BF16),
            pltpu.VMEM((early, halo_rows, cw), BF16),
            dma((3,)),
            dma((9,)),
            dma((2, rounds)),
            dma((2, rounds)),
            dma((chunks, rounds)),
            dma((chunks, rounds)),
            dma((chunks - early, rounds)),
            dma((chunks - early, rounds)),
            dma((early, rounds)),
            dma((early, rounds)),
            dma((1,)),
            dma((1,)),
            dma((early,)),
            dma((early,)),
            dma((chunks,)),
            dma((chunks,)),
            pltpu.SemaphoreType.REGULAR,
        ],
        compiler_params=pltpu.CompilerParams(
            collective_id=0, has_side_effects=True, vmem_limit_bytes=32 * 2**20
        ),
    )(*args)


def solution(mesh):
    in_specs = (
        P("segment", "dom", None),
        P("segment", "dom", None),
        P("segment", "dom", None),
        P("segment", None, None, None),
        P("segment", None, None, None),
        P("dom", None),
        P("dom", None, None),
        P("dom"),
        P("dom", None),
        P("dom", None, None),
        P("dom", None),
    )
    out_specs = P("segment", "dom", None)
    return jax.shard_map(
        on_device, mesh=mesh, in_specs=in_specs, out_specs=out_specs, check_vma=False
    )
```

```python
import functools

import jax
import jax.numpy as jnp
from jax import lax
from jax.experimental import pallas as pl
from jax.experimental.pallas import tpu as pltpu
from jax.sharding import PartitionSpec as P

MESH = pl.DeviceIdType.MESH
BF16 = jnp.bfloat16
F32 = jnp.float32
BLOCK = 128


def dot(a, b):
    return jnp.dot(a, b, preferred_element_type=F32)


def dot_t(a, b):
    return lax.dot_general(a, b, (((1,), (1,)), ((), ())), preferred_element_type=F32)


def silu_grad(z):
    half = 0.5 * jnp.tanh(0.5 * z)
    return (0.5 + half) + z * (0.25 - half * half)


def kernel(
    segments,
    bits,
    early,
    chunks,
    held,
    gate,
    x_in_h,
    x_mid_h,
    dout_h,
    w_in_h,
    w_out_h,
    tile_index_h,
    tile_values_h,
    tile_count,
    coupling_h,
    bound_index_h,
    bound_count_h,
    out_h,
    tile_index,
    bound_count,
    bound_index,
    x_mid,
    x_in,
    dout,
    w_in,
    w_out,
    tiles,
    coup,
    adj,
    adj_t,
    coup_t,
    sel_t,
    sent,
    halo,
    dm,
    base,
    ds,
    zs,
    dg1,
    inc1,
    dg0,
    inc0,
    dxb,
    base_out,
    base_in,
    dg1_in,
    dm_in,
    dgx,
    incx,
    small_sem,
    load_sem,
    halo_send,
    halo_recv,
    g1_send,
    g1_recv,
    g0_send,
    g0_recv,
    gx_send,
    gx_recv,
    base_send,
    base_recv,
    dg_send,
    dg_recv,
    out_send,
    out_recv,
    turn,
):
    seg = lax.axis_index("segment")
    me = lax.axis_index("dom")
    core = lax.rem(me, 2)
    nodes, width = x_mid.shape
    rounds = len(bits)
    rows = bound_index.shape[2]
    slots = tile_values_h.shape[0]
    blocks = nodes // BLOCK
    cw = width // chunks
    partners = []
    for bit in bits:
        mask = 1 << bit
        partners.append(me + mask - 2 * mask * lax.rem(me // mask, 2))
    order = list(range(rounds))[::-1]

    barrier = pltpu.get_barrier_semaphore()
    for r in order:
        pl.semaphore_signal(
            barrier, inc=1, device_id=(seg, partners[r]), device_id_type=MESH
        )

    @pl.when(seg > 0)
    def _():
        pl.semaphore_signal(barrier, inc=1, device_id=(seg - 1, me), device_id_type=MESH)

    @pl.when(seg < segments - 1)
    def _():
        pl.semaphore_signal(barrier, inc=1, device_id=(seg + 1, me), device_id_type=MESH)

    smalls = [
        pltpu.make_async_copy(src, dst, small_sem.at[i])
        for i, (src, dst) in enumerate(
            (
                (bound_index_h, bound_index),
                (bound_count_h, bound_count),
                (tile_index_h, tile_index),
            )
        )
    ]
    loads = [
        pltpu.make_async_copy(src, dst, load_sem.at[i])
        for i, (src, dst) in enumerate(
            (
                (x_mid_h.at[0], x_mid),
                (x_in_h.at[0], x_in),
                (tile_values_h, tiles.at[pl.ds(0, slots)]),
                (coupling_h, coup),
                (dout_h.at[0], dout),
                (w_out_h.at[0, 1], w_out.at[1]),
                (w_in_h.at[0, 1], w_in.at[1]),
                (w_in_h.at[0, 0], w_in.at[0]),
                (w_out_h.at[0, 0], w_out.at[0]),
            )
        )
    ]
    for small in smalls[:2]:
        small.start()
    loads[0].start()
    smalls[2].start()

    def cols(c):
        return slice(c * cw, (c + 1) * cw)

    def piece(r):
        return pl.ds(r * rows, rows)

    for small in smalls[:2]:
        small.wait()
    places = []
    picks = []
    for r in range(rounds):
        row = bound_index[r]
        lane = lax.broadcasted_iota(jnp.int32, (1, rows), 1)
        row = jnp.where(lane < bound_count[0, r], row, -1)
        places.append(row)
        square = lax.broadcasted_iota(jnp.int32, (rows, rows), 0) == lax.broadcasted_iota(
            jnp.int32, (rows, rows), 1
        )
        column = jnp.sum(jnp.where(square, row.astype(F32), 0.0), axis=1, keepdims=True)
        picks.append(
            jnp.where(
                lax.broadcasted_iota(jnp.int32, (rows, nodes), 1).astype(F32) == column, 1.0, 0.0
            ).astype(BF16)
        )
    sel = jnp.concatenate(picks, axis=0)
    for load in loads[1:]:
        load.start()

    loads[0].wait()
    sent[0] = dot(sel, x_mid[...]).astype(BF16)

    neighbours = jnp.minimum(seg, 1) + jnp.minimum(segments - 1 - seg, 1)
    pl.semaphore_wait(barrier, rounds + neighbours)

    def exchange(src, dst, r, send_sem, recv_sem):
        return pltpu.make_async_remote_copy(
            src_ref=src,
            dst_ref=dst,
            send_sem=send_sem,
            recv_sem=recv_sem,
            device_id=(seg, partners[r]),
            device_id_type=MESH,
        )

    def to_previous(src, dst, send_sem, recv_sem):
        return pltpu.make_async_remote_copy(
            src_ref=src,
            dst_ref=dst,
            send_sem=send_sem,
            recv_sem=recv_sem,
            device_id=(jnp.maximum(seg - 1, 0), me),
            device_id_type=MESH,
        )

    def grads(c, dg, inc, send_sem, recv_sem):
        return [
            exchange(
                dg.at[c, piece(r)], inc.at[c, piece(r)], r, send_sem.at[c, r], recv_sem.at[c, r]
            )
            for r in range(rounds)
        ]

    halos = [
        [
            exchange(
                sent.at[k, piece(r)], halo.at[k, piece(r)], r, halo_send.at[k, r], halo_recv.at[k, r]
            )
            for r in range(rounds)
        ]
        for k in range(2)
    ]
    copies1 = [grads(c, dg1, inc1, g1_send, g1_recv) for c in range(chunks)]
    copies0 = [grads(c, dg0, inc0, g0_send, g0_recv) for c in range(chunks - early)]
    copiesx = [grads(c, dgx, incx, gx_send, gx_recv) for c in range(early)]
    base_copy = to_previous(base_out, base_in, base_send.at[0], base_recv.at[0])
    dg_copies = [
        to_previous(dg1.at[c], dg1_in.at[c], dg_send.at[c], dg_recv.at[c]) for c in range(early)
    ]
    outs = [
        to_previous(
            dxb.at[c],
            dm_in.at[c] if c < early else out_h.at[0, :, pl.ds(c * cw, cw)],
            out_send.at[c],
            out_recv.at[c],
        )
        for c in range(chunks)
    ]

    def start_all(copies):
        for r in order:
            copies[r].start()

    def receive_all(copies):
        for r in order:
            copies[r].wait_recv()

    start_all(halos[0])
    for r in range(rounds):
        sel_t[:, r * rows : (r + 1) * rows] = jnp.where(
            lax.broadcasted_iota(jnp.int32, (nodes, rows), 0) == places[r], 1.0, 0.0
        ).astype(BF16)
    loads[1].wait()
    sent[1] = dot(sel, x_in[...]).astype(BF16)

    tiles[slots] = jnp.zeros((BLOCK, BLOCK), BF16)
    loads[2].wait()
    smalls[2].wait()
    keys = [
        jnp.where(t < tile_count[0], tile_index[0, t] * blocks + tile_index[1, t], -1)
        for t in range(slots)
    ]
    for a in range(blocks):
        for b in range(blocks):
            slot = jnp.int32(slots)
            for t in range(slots):
                slot = jnp.where(keys[t] == a * blocks + b, t, slot)
            tile = tiles[slot]
            adj[a * BLOCK : (a + 1) * BLOCK, b * BLOCK : (b + 1) * BLOCK] = tile
            adj_t[b * BLOCK : (b + 1) * BLOCK, a * BLOCK : (a + 1) * BLOCK] = tile.T
    loads[3].wait()
    coup_t[...] = coup[...].T

    merged = dot(adj[...], x_mid[...]).astype(BF16)
    loads[4].wait()
    loads[5].wait()
    ds[...] = dot_t(dout[...], w_out[1])
    loads[6].wait()
    zs[1] = dot(merged, w_in[1])
    merged = dot(adj[...], x_in[...]).astype(BF16)
    loads[7].wait()
    loads[8].wait()
    zs[0] = dot(merged, w_in[0])
    start_all(halos[1])

    receive_all(halos[0])
    far = dot(halo[0], w_in[1]).astype(BF16)
    z = zs[1] + dot(coup_t[...], far)
    dz = (ds[...] * silu_grad(z)).astype(BF16)

    for c in range(chunks):
        if c % 2 == 0:
            wide = dot_t(dz, w_in[1, c * cw : (c + 2) * cw, :]).astype(BF16)
            dm[:, c * cw : (c + 2) * cw] = wide
            grad = dot(coup[...], wide).astype(BF16)
        dg1[c] = grad[:, (c % 2) * cw : (c % 2 + 1) * cw]
        start_all(copies1[c])
        if c < early:

            @pl.when(seg > 0)
            def _():
                dg_copies[c].start()

    base[...] = dout[...].astype(F32) + dot(adj_t[...], dm[...])
    base_out[...] = base[:, : early * cw].astype(BF16)

    @pl.when(seg > 0)
    def _():
        base_copy.start()

    ds[...] = dot_t(base[...].astype(BF16), w_out[0])
    receive_all(halos[1])
    far = dot(halo[1], w_in[0]).astype(BF16)
    zs[0] = silu_grad(zs[0] + dot(coup_t[...], far))
    far = None
    for c in range(chunks):
        receive_all(copies1[c])
        term = dot_t(inc1[c], w_out[0, :, cols(c)])
        far = term if far is None else far + term
    dz = ((ds[...] + dot(sel_t[...], far.astype(BF16))) * zs[0]).astype(BF16)

    def push(c):
        @pl.when(seg > 0)
        def _():
            outs[c].start()

    def without_far(c):
        got = (base[:, cols(c)] + dot(sel_t[...], inc1[c])).astype(BF16).astype(F32)
        return got + dot(adj_t[...], dm[:, cols(c)])

    first = dot_t(dz, w_in[0, : (early + 1) * cw, :]).astype(BF16)
    for c in range(early):
        dxb[c] = first[:, cols(c)]
        push(c)
    for c in range(early, chunks):
        if c == early:
            part = first[:, cols(c)]
            dm[:, cols(c)] = part
            dg0[0] = dot(coup[...], part).astype(BF16)
        elif c == early + 1:
            wide = dot_t(dz, w_in[0, c * cw :, :]).astype(BF16)
            dm[:, c * cw :] = wide
            grad = dot(coup[...], wide).astype(BF16)
        if c > early:
            k = c - early - 1
            dg0[c - early] = grad[:, k * cw : (k + 1) * cw]
        start_all(copies0[c - early])
        if c < early:
            dxb[c] = without_far(c).astype(BF16)
            push(c)
    for c in range(early, chunks):
        base[:, cols(c)] = without_far(c)
    for c in range(early, chunks):
        receive_all(copies0[c - early])
        dxb[c] = (base[:, cols(c)] + dot(sel_t[...], inc0[c - early])).astype(BF16)

        @pl.when((seg > 0) & ((core == 0) | (c < chunks - held)))
        def _():
            outs[c].start()

    @pl.when(seg == segments - 1)
    def _():
        out_h[...] = jnp.zeros(out_h.shape, BF16)

    @pl.when(seg < segments - 1)
    def _():
        for c in range(early):
            outs[c].wait_recv()
            dg_copies[c].wait_recv()
            dgx[c] = (dg1_in[c].astype(F32) + dot(coup[...], dm_in[c])).astype(BF16)
            start_all(copiesx[c])
            if c == 0:
                base_copy.wait_recv()
            base[:, cols(c)] = base_in[:, cols(c)].astype(F32) + dot(adj_t[...], dm_in[c])

    @pl.when((seg > 0) & (core == 0))
    def _():
        for c in range(gate + 1):
            outs[c].wait_send()
        pl.semaphore_signal(turn, inc=1, device_id=(seg, partners[0]), device_id_type=MESH)

    @pl.when((seg > 0) & (core > 0))
    def _():
        pl.semaphore_wait(turn, 1)
        for c in range(chunks - held, chunks):
            outs[c].start()

    @pl.when(seg < segments - 1)
    def _():
        for c in range(early):
            receive_all(copiesx[c])
            out_h[0, :, cols(c)] = (base[:, cols(c)] + dot(sel_t[...], incx[c])).astype(BF16)
        for c in range(early):
            for copy in copiesx[c]:
                copy.wait_send()
        for c in range(early, chunks):
            outs[c].wait_recv()

    for copies in halos + copies1 + copies0:
        for copy in copies:
            copy.wait_send()

    @pl.when(seg > 0)
    def _():
        base_copy.wait_send()
        for copy in dg_copies + outs[gate + 1 :]:
            copy.wait_send()

    @pl.when((seg > 0) & (core > 0))
    def _():
        for copy in outs[: gate + 1]:
            copy.wait_send()


def on_device(*args):
    (states_in, _, _, w_in, w_out, tile_index, tile_values, _, coupling, bound_index, _) = args
    args = args[:5] + (tile_index.T,) + args[6:9] + (bound_index.transpose(1, 0, 2), args[10])
    _, nodes, width = states_in.shape
    rounds, rows = bound_index.shape[1:]
    halo_rows = rounds * rows
    slots = tile_values.shape[0]
    segments = lax.axis_size("segment")
    levels = lax.axis_size("dom").bit_length() - 1
    bits = tuple(r * (levels - 1) // (rounds - 1) for r in range(rounds))
    early, chunks, held, gate = 1, 4, 1, 2
    cw = width // chunks
    whole = pl.BlockSpec(memory_space=pltpu.HBM)
    dma = pltpu.SemaphoreType.DMA
    args = tuple(
        a if i == 7 else pltpu.with_memory_space_constraint(a, pltpu.HBM) for i, a in enumerate(args)
    )
    return pl.pallas_call(
        functools.partial(kernel, segments, bits, early, chunks, held, gate),
        out_shape=jax.ShapeDtypeStruct(states_in.shape, BF16),
        in_specs=[whole] * 7 + [pl.BlockSpec(memory_space=pltpu.SMEM)] + [whole] * 3,
        out_specs=pl.BlockSpec(memory_space=pltpu.VMEM),
        scratch_shapes=[
            pltpu.SMEM(args[5].shape, jnp.int32),
            pltpu.SMEM(args[10].shape, jnp.int32),
            pltpu.VMEM(args[9].shape, jnp.int32),
            pltpu.VMEM((nodes, width), BF16),
            pltpu.VMEM((nodes, width), BF16),
            pltpu.VMEM((nodes, width), BF16),
            pltpu.VMEM(w_in.shape[1:], BF16),
            pltpu.VMEM(w_out.shape[1:], BF16),
            pltpu.VMEM((slots + 1,) + tile_values.shape[1:], BF16),
            pltpu.VMEM((halo_rows, nodes), BF16),
            pltpu.VMEM((nodes, nodes), BF16),
            pltpu.VMEM((nodes, nodes), BF16),
            pltpu.VMEM((nodes, halo_rows), BF16),
            pltpu.VMEM((nodes, halo_rows), BF16),
            pltpu.VMEM((2, halo_rows, width), BF16),
            pltpu.VMEM((2, halo_rows, width), BF16),
            pltpu.VMEM((nodes, width), BF16),
            pltpu.VMEM((nodes, width), F32),
            pltpu.VMEM((nodes, width), F32),
            pltpu.VMEM((2, nodes, width), F32),
            pltpu.VMEM((chunks, halo_rows, cw), BF16),
            pltpu.VMEM((chunks, halo_rows, cw), BF16),
            pltpu.VMEM((chunks - early, halo_rows, cw), BF16),
            pltpu.VMEM((chunks - early, halo_rows, cw), BF16),
            pltpu.VMEM((chunks, nodes, cw), BF16),
            pltpu.VMEM((nodes, early * cw), BF16),
            pltpu.VMEM((nodes, early * cw), BF16),
            pltpu.VMEM((early, halo_rows, cw), BF16),
            pltpu.VMEM((early, nodes, cw), BF16),
            pltpu.VMEM((early, halo_rows, cw), BF16),
            pltpu.VMEM((early, halo_rows, cw), BF16),
            dma((3,)),
            dma((9,)),
            dma((2, rounds)),
            dma((2, rounds)),
            dma((chunks, rounds)),
            dma((chunks, rounds)),
            dma((chunks - early, rounds)),
            dma((chunks - early, rounds)),
            dma((early, rounds)),
            dma((early, rounds)),
            dma((1,)),
            dma((1,)),
            dma((early,)),
            dma((early,)),
            dma((chunks,)),
            dma((chunks,)),
            pltpu.SemaphoreType.REGULAR,
        ],
        compiler_params=pltpu.CompilerParams(
            collective_id=0, has_side_effects=True, vmem_limit_bytes=32 * 2**20
        ),
    )(*args)


def solution(mesh):
    in_specs = (
        P("segment", "dom", None),
        P("segment", "dom", None),
        P("segment", "dom", None),
        P("segment", None, None, None),
        P("segment", None, None, None),
        P("dom", None),
        P("dom", None, None),
        P("dom"),
        P("dom", None),
        P("dom", None, None),
        P("dom", None),
    )
    out_specs = P("segment", "dom", None)
    return jax.shard_map(
        on_device, mesh=mesh, in_specs=in_specs, out_specs=out_specs, check_vma=False
    )
```

```python
import functools

import jax
import jax.numpy as jnp
from jax import lax
from jax.experimental import pallas as pl
from jax.experimental.pallas import tpu as pltpu
from jax.sharding import PartitionSpec as P

MESH = pl.DeviceIdType.MESH
BF16 = jnp.bfloat16
F32 = jnp.float32
BLOCK = 128


def dot(a, b):
    return jnp.dot(a, b, preferred_element_type=F32)


def dot_t(a, b):
    return lax.dot_general(a, b, (((1,), (1,)), ((), ())), preferred_element_type=F32)


def silu_grad(z):
    half = 0.5 * jnp.tanh(0.5 * z)
    return (0.5 + half) + z * (0.25 - half * half)


def kernel(
    segments,
    bits,
    early,
    chunks,
    held,
    gate,
    x_in_h,
    x_mid_h,
    dout_h,
    w_in_h,
    w_out_h,
    tile_index_h,
    tile_values_h,
    tile_count,
    coupling_h,
    bound_index_h,
    bound_count_h,
    out_h,
    tile_index,
    bound_count,
    bound_index,
    x_mid,
    x_in,
    dout,
    w_in,
    w_out,
    tiles,
    coup,
    adj,
    adj_t,
    coup_t,
    sel_t,
    sent,
    halo,
    dm,
    base,
    ds,
    zs,
    dg1,
    inc1,
    dg0,
    inc0,
    dxb,
    base_out,
    base_in,
    dg1_in,
    dm_in,
    dgx,
    incx,
    small_sem,
    load_sem,
    halo_send,
    halo_recv,
    g1_send,
    g1_recv,
    g0_send,
    g0_recv,
    gx_send,
    gx_recv,
    base_send,
    base_recv,
    dg_send,
    dg_recv,
    out_send,
    out_recv,
    turn,
):
    seg = lax.axis_index("segment")
    me = lax.axis_index("dom")
    core = lax.rem(me, 2)
    nodes, width = x_mid.shape
    rounds = len(bits)
    rows = bound_index.shape[2]
    slots = tile_values_h.shape[0]
    blocks = nodes // BLOCK
    cw = width // chunks
    partners = []
    for bit in bits:
        mask = 1 << bit
        partners.append(me + mask - 2 * mask * lax.rem(me // mask, 2))
    order = list(range(rounds))[::-1]

    barrier = pltpu.get_barrier_semaphore()
    for r in order:
        pl.semaphore_signal(
            barrier, inc=1, device_id=(seg, partners[r]), device_id_type=MESH
        )

    @pl.when(seg > 0)
    def _():
        pl.semaphore_signal(barrier, inc=1, device_id=(seg - 1, me), device_id_type=MESH)

    @pl.when(seg < segments - 1)
    def _():
        pl.semaphore_signal(barrier, inc=1, device_id=(seg + 1, me), device_id_type=MESH)

    smalls = [
        pltpu.make_async_copy(src, dst, small_sem.at[i])
        for i, (src, dst) in enumerate(
            (
                (bound_index_h, bound_index),
                (bound_count_h, bound_count),
                (tile_index_h, tile_index),
            )
        )
    ]
    loads = [
        pltpu.make_async_copy(src, dst, load_sem.at[i])
        for i, (src, dst) in enumerate(
            (
                (x_mid_h.at[0], x_mid),
                (x_in_h.at[0], x_in),
                (tile_values_h, tiles.at[pl.ds(0, slots)]),
                (coupling_h, coup),
                (dout_h.at[0], dout),
                (w_out_h.at[0, 1], w_out.at[1]),
                (w_in_h.at[0, 1], w_in.at[1]),
                (w_in_h.at[0, 0], w_in.at[0]),
                (w_out_h.at[0, 0], w_out.at[0]),
            )
        )
    ]
    for small in smalls[:2]:
        small.start()
    loads[0].start()
    smalls[2].start()

    def cols(c):
        return slice(c * cw, (c + 1) * cw)

    def piece(r):
        return pl.ds(r * rows, rows)

    for small in smalls[:2]:
        small.wait()
    places = []
    picks = []
    for r in range(rounds):
        row = bound_index[r]
        lane = lax.broadcasted_iota(jnp.int32, (1, rows), 1)
        row = jnp.where(lane < bound_count[0, r], row, -1)
        places.append(row)
        square = lax.broadcasted_iota(jnp.int32, (rows, rows), 0) == lax.broadcasted_iota(
            jnp.int32, (rows, rows), 1
        )
        column = jnp.sum(jnp.where(square, row.astype(F32), 0.0), axis=1, keepdims=True)
        picks.append(
            jnp.where(
                lax.broadcasted_iota(jnp.int32, (rows, nodes), 1).astype(F32) == column, 1.0, 0.0
            ).astype(BF16)
        )
    sel = jnp.concatenate(picks, axis=0)
    for load in loads[1:]:
        load.start()

    loads[0].wait()
    sent[0] = dot(sel, x_mid[...]).astype(BF16)

    neighbours = jnp.minimum(seg, 1) + jnp.minimum(segments - 1 - seg, 1)
    pl.semaphore_wait(barrier, rounds + neighbours)

    def exchange(src, dst, r, send_sem, recv_sem):
        return pltpu.make_async_remote_copy(
            src_ref=src,
            dst_ref=dst,
            send_sem=send_sem,
            recv_sem=recv_sem,
            device_id=(seg, partners[r]),
            device_id_type=MESH,
        )

    def to_previous(src, dst, send_sem, recv_sem):
        return pltpu.make_async_remote_copy(
            src_ref=src,
            dst_ref=dst,
            send_sem=send_sem,
            recv_sem=recv_sem,
            device_id=(jnp.maximum(seg - 1, 0), me),
            device_id_type=MESH,
        )

    def grads(c, dg, inc, send_sem, recv_sem):
        return [
            exchange(
                dg.at[c, piece(r)], inc.at[c, piece(r)], r, send_sem.at[c, r], recv_sem.at[c, r]
            )
            for r in range(rounds)
        ]

    halos = [
        [
            exchange(
                sent.at[k, piece(r)], halo.at[k, piece(r)], r, halo_send.at[k, r], halo_recv.at[k, r]
            )
            for r in range(rounds)
        ]
        for k in range(2)
    ]
    copies1 = [grads(c, dg1, inc1, g1_send, g1_recv) for c in range(chunks)]
    copies0 = [grads(c, dg0, inc0, g0_send, g0_recv) for c in range(chunks - early)]
    copiesx = [grads(c, dgx, incx, gx_send, gx_recv) for c in range(early)]
    base_copy = to_previous(base_out, base_in, base_send.at[0], base_recv.at[0])
    dg_copies = [
        to_previous(dg1.at[c], dg1_in.at[c], dg_send.at[c], dg_recv.at[c]) for c in range(early)
    ]
    outs = [
        to_previous(
            dxb.at[c],
            dm_in.at[c] if c < early else out_h.at[0, :, pl.ds(c * cw, cw)],
            out_send.at[c],
            out_recv.at[c],
        )
        for c in range(chunks)
    ]

    def start_all(copies):
        for r in order:
            copies[r].start()

    def receive_all(copies):
        for r in order:
            copies[r].wait_recv()

    start_all(halos[0])
    for r in range(rounds):
        sel_t[:, r * rows : (r + 1) * rows] = jnp.where(
            lax.broadcasted_iota(jnp.int32, (nodes, rows), 0) == places[r], 1.0, 0.0
        ).astype(BF16)
    loads[1].wait()
    sent[1] = dot(sel, x_in[...]).astype(BF16)

    tiles[slots] = jnp.zeros((BLOCK, BLOCK), BF16)
    loads[2].wait()
    smalls[2].wait()
    keys = [
        jnp.where(t < tile_count[0], tile_index[0, t] * blocks + tile_index[1, t], -1)
        for t in range(slots)
    ]
    for a in range(blocks):
        for b in range(blocks):
            slot = jnp.int32(slots)
            for t in range(slots):
                slot = jnp.where(keys[t] == a * blocks + b, t, slot)
            tile = tiles[slot]
            adj[a * BLOCK : (a + 1) * BLOCK, b * BLOCK : (b + 1) * BLOCK] = tile
            adj_t[b * BLOCK : (b + 1) * BLOCK, a * BLOCK : (a + 1) * BLOCK] = tile.T
    loads[3].wait()
    coup_t[...] = coup[...].T

    merged = dot(adj[...], x_mid[...]).astype(BF16)
    loads[4].wait()
    loads[5].wait()
    ds[...] = dot_t(dout[...], w_out[1])
    loads[6].wait()
    zs[1] = dot(merged, w_in[1])
    merged = dot(adj[...], x_in[...]).astype(BF16)
    loads[7].wait()
    loads[8].wait()
    zs[0] = dot(merged, w_in[0])
    start_all(halos[1])

    receive_all(halos[0])
    far = dot(halo[0], w_in[1]).astype(BF16)
    z = zs[1] + dot(coup_t[...], far)
    dz = (ds[...] * silu_grad(z)).astype(BF16)

    for c in range(chunks):
        if c == 0:
            wide = dot_t(dz, w_in[1]).astype(BF16)
            dm[...] = wide
            grad = dot(coup[...], wide).astype(BF16)
        dg1[c] = grad[:, cols(c)]
        start_all(copies1[c])
        if c < early:

            @pl.when(seg > 0)
            def _():
                dg_copies[c].start()

    base[...] = dout[...].astype(F32) + dot(adj_t[...], dm[...])
    base_out[...] = base[:, : early * cw].astype(BF16)

    @pl.when(seg > 0)
    def _():
        base_copy.start()

    ds[...] = dot_t(base[...].astype(BF16), w_out[0])
    receive_all(halos[1])
    far = dot(halo[1], w_in[0]).astype(BF16)
    zs[0] = silu_grad(zs[0] + dot(coup_t[...], far))
    far = None
    for c in range(chunks):
        receive_all(copies1[c])
        term = dot_t(inc1[c], w_out[0, :, cols(c)])
        far = term if far is None else far + term
    dz = ((ds[...] + dot(sel_t[...], far.astype(BF16))) * zs[0]).astype(BF16)

    def push(c):
        @pl.when(seg > 0)
        def _():
            outs[c].start()

    def without_far(c):
        got = (base[:, cols(c)] + dot(sel_t[...], inc1[c])).astype(BF16).astype(F32)
        return got + dot(adj_t[...], dm[:, cols(c)])

    first = dot_t(dz, w_in[0, : (early + 1) * cw, :]).astype(BF16)
    for c in range(early):
        dxb[c] = first[:, cols(c)]
        push(c)
    for c in range(early, chunks):
        if c == early:
            part = first[:, cols(c)]
            dm[:, cols(c)] = part
            dg0[0] = dot(coup[...], part).astype(BF16)
        elif c == early + 1:
            wide = dot_t(dz, w_in[0, c * cw :, :]).astype(BF16)
            dm[:, c * cw :] = wide
            grad = dot(coup[...], wide).astype(BF16)
        if c > early:
            k = c - early - 1
            dg0[c - early] = grad[:, k * cw : (k + 1) * cw]
        start_all(copies0[c - early])
        if c < early:
            dxb[c] = without_far(c).astype(BF16)
            push(c)
    for c in range(early, chunks):
        base[:, cols(c)] = without_far(c)
    for c in range(early, chunks):
        receive_all(copies0[c - early])
        dxb[c] = (base[:, cols(c)] + dot(sel_t[...], inc0[c - early])).astype(BF16)

        @pl.when((seg > 0) & ((core == 0) | (c < chunks - held)))
        def _():
            outs[c].start()

    @pl.when(seg == segments - 1)
    def _():
        out_h[...] = jnp.zeros(out_h.shape, BF16)

    @pl.when(seg < segments - 1)
    def _():
        for c in range(early):
            outs[c].wait_recv()
            dg_copies[c].wait_recv()
            dgx[c] = (dg1_in[c].astype(F32) + dot(coup[...], dm_in[c])).astype(BF16)
            start_all(copiesx[c])
            if c == 0:
                base_copy.wait_recv()
            base[:, cols(c)] = base_in[:, cols(c)].astype(F32) + dot(adj_t[...], dm_in[c])

    @pl.when((seg > 0) & (core == 0))
    def _():
        for c in range(gate + 1):
            outs[c].wait_send()
        pl.semaphore_signal(turn, inc=1, device_id=(seg, partners[0]), device_id_type=MESH)

    @pl.when((seg > 0) & (core > 0))
    def _():
        pl.semaphore_wait(turn, 1)
        for c in range(chunks - held, chunks):
            outs[c].start()

    @pl.when(seg < segments - 1)
    def _():
        for c in range(early):
            receive_all(copiesx[c])
            out_h[0, :, cols(c)] = (base[:, cols(c)] + dot(sel_t[...], incx[c])).astype(BF16)
        for c in range(early):
            for copy in copiesx[c]:
                copy.wait_send()
        for c in range(early, chunks):
            outs[c].wait_recv()

    for copies in halos + copies1 + copies0:
        for copy in copies:
            copy.wait_send()

    @pl.when(seg > 0)
    def _():
        base_copy.wait_send()
        for copy in dg_copies + outs[gate + 1 :]:
            copy.wait_send()

    @pl.when((seg > 0) & (core > 0))
    def _():
        for copy in outs[: gate + 1]:
            copy.wait_send()


def on_device(*args):
    (states_in, _, _, w_in, w_out, tile_index, tile_values, _, coupling, bound_index, _) = args
    args = args[:5] + (tile_index.T,) + args[6:9] + (bound_index.transpose(1, 0, 2), args[10])
    _, nodes, width = states_in.shape
    rounds, rows = bound_index.shape[1:]
    halo_rows = rounds * rows
    slots = tile_values.shape[0]
    segments = lax.axis_size("segment")
    levels = lax.axis_size("dom").bit_length() - 1
    bits = tuple(r * (levels - 1) // (rounds - 1) for r in range(rounds))
    early, chunks, held, gate = 1, 4, 1, 2
    cw = width // chunks
    whole = pl.BlockSpec(memory_space=pltpu.HBM)
    dma = pltpu.SemaphoreType.DMA
    args = tuple(
        a if i == 7 else pltpu.with_memory_space_constraint(a, pltpu.HBM) for i, a in enumerate(args)
    )
    return pl.pallas_call(
        functools.partial(kernel, segments, bits, early, chunks, held, gate),
        out_shape=jax.ShapeDtypeStruct(states_in.shape, BF16),
        in_specs=[whole] * 7 + [pl.BlockSpec(memory_space=pltpu.SMEM)] + [whole] * 3,
        out_specs=pl.BlockSpec(memory_space=pltpu.VMEM),
        scratch_shapes=[
            pltpu.SMEM(args[5].shape, jnp.int32),
            pltpu.SMEM(args[10].shape, jnp.int32),
            pltpu.VMEM(args[9].shape, jnp.int32),
            pltpu.VMEM((nodes, width), BF16),
            pltpu.VMEM((nodes, width), BF16),
            pltpu.VMEM((nodes, width), BF16),
            pltpu.VMEM(w_in.shape[1:], BF16),
            pltpu.VMEM(w_out.shape[1:], BF16),
            pltpu.VMEM((slots + 1,) + tile_values.shape[1:], BF16),
            pltpu.VMEM((halo_rows, nodes), BF16),
            pltpu.VMEM((nodes, nodes), BF16),
            pltpu.VMEM((nodes, nodes), BF16),
            pltpu.VMEM((nodes, halo_rows), BF16),
            pltpu.VMEM((nodes, halo_rows), BF16),
            pltpu.VMEM((2, halo_rows, width), BF16),
            pltpu.VMEM((2, halo_rows, width), BF16),
            pltpu.VMEM((nodes, width), BF16),
            pltpu.VMEM((nodes, width), F32),
            pltpu.VMEM((nodes, width), F32),
            pltpu.VMEM((2, nodes, width), F32),
            pltpu.VMEM((chunks, halo_rows, cw), BF16),
            pltpu.VMEM((chunks, halo_rows, cw), BF16),
            pltpu.VMEM((chunks - early, halo_rows, cw), BF16),
            pltpu.VMEM((chunks - early, halo_rows, cw), BF16),
            pltpu.VMEM((chunks, nodes, cw), BF16),
            pltpu.VMEM((nodes, early * cw), BF16),
            pltpu.VMEM((nodes, early * cw), BF16),
            pltpu.VMEM((early, halo_rows, cw), BF16),
            pltpu.VMEM((early, nodes, cw), BF16),
            pltpu.VMEM((early, halo_rows, cw), BF16),
            pltpu.VMEM((early, halo_rows, cw), BF16),
            dma((3,)),
            dma((9,)),
            dma((2, rounds)),
            dma((2, rounds)),
            dma((chunks, rounds)),
            dma((chunks, rounds)),
            dma((chunks - early, rounds)),
            dma((chunks - early, rounds)),
            dma((early, rounds)),
            dma((early, rounds)),
            dma((1,)),
            dma((1,)),
            dma((early,)),
            dma((early,)),
            dma((chunks,)),
            dma((chunks,)),
            pltpu.SemaphoreType.REGULAR,
        ],
        compiler_params=pltpu.CompilerParams(
            collective_id=0, has_side_effects=True, vmem_limit_bytes=32 * 2**20
        ),
    )(*args)


def solution(mesh):
    in_specs = (
        P("segment", "dom", None),
        P("segment", "dom", None),
        P("segment", "dom", None),
        P("segment", None, None, None),
        P("segment", None, None, None),
        P("dom", None),
        P("dom", None, None),
        P("dom"),
        P("dom", None),
        P("dom", None, None),
        P("dom", None),
    )
    out_specs = P("segment", "dom", None)
    return jax.shard_map(
        on_device, mesh=mesh, in_specs=in_specs, out_specs=out_specs, check_vma=False
    )
```
